256 devices in a mesh: dp: 8 (over x, core), expert: 32 (over z, y).
Axes of the slice: x: 4, y: 4, z: 8, core: 2. Of those that a mesh axis runs over, the one named last changes fastest.
Arguments:
- tokens: bfloat16 [32768, 2048], P(('dp', 'expert')), may hold values from -6 to 6
- routes: int32 [32768, 2], P(('dp', 'expert')), may hold values from 0 to 31, all different within a row; in each aligned block of 128 rows (0 to 127, 128 to 255, ...) at most 12 rows name the same one
- gates: float32 [32768, 2], P(('dp', 'expert')), may hold values from 0.25 to 1
- keep: int32 [32768], P(('dp', 'expert')), may hold values 0 or 1
- cotangent: bfloat16 [32768, 2048], P(('dp', 'expert')), may hold values from -6 to 6
- w_gate: bfloat16 [32, 2048, 768], P('expert'), may hold values from -0.125 to 0.125
- w_up: bfloat16 [32, 2048, 768], P('expert'), may hold values from -0.125 to 0.125
- w_down: bfloat16 [32, 768, 2048], P('expert'), may hold values from -0.21875 to 0.21875
Outputs:
- token_grads: bfloat16 [32768, 2048], P(('dp', 'expert'))
- expert_grads: float32 [32, 2048, 2304], P('expert', 'dp')
The draws below stay inside these ranges and needn't reach their ends.
Inputs may be any that keep to these rules, and one draw needn't show every extreme that they name: `routes`: the 2 experts of a token differ. Among the 128 tokens of one device, no expert is named more than 12 times, a bound that some block reaches.
All inputs are finite; a program needn't handle non-finite values. No bound on the sum of `keep` on one device may be relied on, other than what follows from the above.
Results may differ from the reference program's by a relative error of at most 0.0061.
Values may be sent and summed in bfloat16 or wider, within the bound.
A program may use at most 128 MiB of HBM per device.

```python
import math
import jax
import jax.numpy as jnp
import numpy as np
from jax import lax

D = 2048
FF = 768
TOPW = 2
TOK_DEV = 128
EXPERTS = 32
CAP = 12
TOKENS = 32768
N_DP = 8
N_EXPERT = 32


def set_ends(values, stream_key, low, high):
    longest = values.shape.index(max(values.shape))
    spots = []
    for shift in (0, 1):
        where = [jax.random.randint(jax.random.fold_in(stream_key, axis), (), 0, length) for axis, length in enumerate(values.shape)]
        where[longest] = (where[longest] + shift) % values.shape[longest]
        spots.append(tuple(where))
    return values.at[spots[0]].set(low).at[spots[1]].set(high)


def level_of(stream_key, dims, shards, smallest, largest):
    level, own = 1.0, jax.random.fold_in(stream_key, 6)
    for position, blocks in shards:
        draws = jnp.exp(jax.random.uniform(jax.random.fold_in(own, position), (blocks,), jnp.float32, smallest / len(shards), largest / len(shards)))
        level = level * jnp.repeat(draws, dims[position] // blocks).reshape([-1 if axis == position else 1 for axis in range(len(dims))])
    return level


def assign_block(stream_key, own, number, rows, amount, top, reach, lean):
    order = jax.random.permutation(stream_key, amount)
    crowded, common = portions_of(amount, rows * top, reach, lean, True), portions_of(amount, rows * top, reach, lean, False)
    places = jnp.arange(amount)

    def named(tallies, turn):
        used = int((tallies > 0).sum())
        fixed = max(1, used // 4)
        passed = fixed + (places - fixed + turn * (used - fixed)) % max(1, amount - fixed)
        return jnp.zeros((amount,), jnp.int32).at[order[jnp.where(places < fixed, places, passed)]].set(jnp.asarray(tallies, jnp.int32))

    tallies = jnp.where(number % 4 == 0, named(crowded, number // 4), named(common, number - number // 4 - 1))
    mixed = jax.random.permutation(jax.random.fold_in(own, 3), amount)
    giver, taker = mixed[0:amount // 2 * 2:2], mixed[1:amount // 2 * 2:2]
    slack = jnp.minimum(tallies[giver] - 1, reach - tallies[taker]) // 2
    slack = jnp.where((giver == order[0]) | (taker == order[0]) | (tallies[taker] == 0), 0, jnp.maximum(slack, 0))
    passed = jax.random.randint(jax.random.fold_in(own, 4), (amount // 2,), 0, 1 << 20) % (slack + 1)
    tallies = tallies.at[giver].add(-passed).at[taker].add(passed)
    members = jnp.searchsorted(jnp.cumsum(tallies), jnp.arange(rows * top), side="right").astype(jnp.int32)
    grid = members.reshape(top, rows).T
    grid = grid[jax.random.permutation(jax.random.fold_in(own, 1), rows)]
    turn = jax.random.randint(jax.random.fold_in(own, 2), (rows, 1), 0, top)
    return jnp.take_along_axis(grid, (jnp.arange(top)[None, :] + turn) % top, axis=1)


def portions_of(count, total, bound, skew, full):
    loads = [(1 << 20) // math.isqrt(standing ** skew) + 1 for standing in range(1, count + 1)]
    largest = bound if full else min(bound, max(-(-total // count), total * loads[0] // sum(loads)))
    least = 1 if total - largest >= count - 1 else 0
    counts, spare = [largest] + [least] * (count - 1), total - largest - least * (count - 1)
    while spare > 0:
        candidates = [i for i in range(1, count) if counts[i] < largest] or [i for i in range(1, count) if counts[i] < bound]
        mass, remaining = sum([loads[i] for i in candidates]), spare
        for i in candidates:
            addition = min(bound - counts[i], max(1, remaining * loads[i] // mass), spare)
            counts[i] = counts[i] + addition
            spare = spare - addition
    return np.array(counts)


def normal_values(stream_key, dims, deviation, limit, cuts=(), kind=jnp.bfloat16):
    gain = level_of(stream_key, dims, cuts, -0.22, 0.18) if cuts else 1.0
    entries = jax.random.normal(stream_key, dims, jnp.float32) * deviation * gain
    return jnp.minimum(jnp.maximum(entries, -limit), limit).astype(kind)


def setup_inputs(seed: int = 0) -> dict:
    streams_of = jax.random.split(jax.random.key(seed), 9)
    tokens = normal_values(streams_of[0], (TOKENS, D), 1.0, 6.0, ((0, 256),))
    routes_keys = jax.random.split(jax.random.fold_in(streams_of[1], 1), TOKENS // TOK_DEV)
    routes_turns = jax.random.permutation(jax.random.fold_in(streams_of[1], 3), TOKENS // TOK_DEV)
    routes = jax.vmap(lambda own, number: assign_block(jax.random.fold_in(streams_of[1], 2), own, number, TOK_DEV, EXPERTS, TOPW, CAP, 1))(routes_keys, routes_turns).reshape((TOKENS, TOPW))
    gates = jnp.clip(0.25 + 0.75 * jax.random.uniform(streams_of[2], (TOKENS, TOPW), jnp.float32) ** level_of(streams_of[2], (TOKENS, TOPW), ((0, 256),), -0.2, 0.2), 0.25, 1.0)
    keep = set_ends((jax.random.randint(streams_of[3], (TOKENS,), 0, 2) < 1).astype(jnp.int32), jax.random.fold_in(streams_of[3], 1), 0, 1)
    cotangent = normal_values(streams_of[4], (TOKENS, D), 1.0, 6.0, ((0, 256),))
    w_gate = normal_values(streams_of[5], (EXPERTS, D, FF), D ** -0.5, 0.125, ((0, 32),))
    w_up = normal_values(streams_of[6], (EXPERTS, D, FF), D ** -0.5, 0.125, ((0, 32),))
    w_down = normal_values(streams_of[7], (EXPERTS, FF, D), FF ** -0.5, 0.21875, ((0, 32),))
    return dict(tokens=tokens, routes=routes, gates=gates, keep=keep, cotangent=cotangent, w_gate=w_gate, w_up=w_up, w_down=w_down)


def logistic_parts(act):
    sigma = jax.nn.sigmoid(act)
    return act * sigma, sigma * (1.0 + act * (1.0 - sigma))


def dot_rows(left, right):
    return lax.dot_general(left, right, (((0,), (0,)), ((), ())), preferred_element_type=jnp.float32)


def dot_back(left, weight):
    return lax.dot_general(left, weight, (((1,), (1,)), ((), ())), preferred_element_type=jnp.float32)


def slot_numbers(routes):
    blocks = routes.reshape(-1, TOK_DEV * TOPW)
    expert_ids = lax.broadcasted_iota(jnp.int32, (1, 1, EXPERTS), 2)
    onehot = (blocks[:, :, None] == expert_ids).astype(jnp.int32)
    before = jnp.cumsum(onehot, axis=1) - onehot
    return jnp.sum(before * onehot, axis=2).reshape(-1, TOPW).astype(jnp.int32)


def reference(tokens, routes, gates, keep, cotangent, w_gate, w_up, w_down):
    slot = slot_numbers(routes)
    tok_ids = lax.broadcasted_iota(jnp.int32, (TOKENS, TOPW), 0)
    device = tok_ids // TOK_DEV
    group = device // N_EXPERT
    source = device % N_EXPERT
    place = (((group * EXPERTS + routes) * N_EXPERT + source) * CAP + slot).reshape(-1).astype(jnp.int32)
    pairs = N_DP * EXPERTS
    per_pair = N_EXPERT * CAP
    repeated = jnp.repeat(tokens, TOPW, axis=0)
    buffer = jnp.zeros((pairs * per_pair, D), tokens.dtype).at[place].set(repeated).reshape(pairs, per_pair, D)
    pair_ids = jnp.arange(pairs, dtype=jnp.int32)

    def expert_hidden(rows, expert):
        gate_act = jnp.dot(rows, w_gate[expert], preferred_element_type=jnp.float32)
        up_act = jnp.dot(rows, w_up[expert], preferred_element_type=jnp.float32)
        silu_val, slope = logistic_parts(gate_act)
        return (silu_val * up_act).astype(jnp.bfloat16)

    def forward(pair):
        expert = pair % EXPERTS
        hidden = expert_hidden(buffer[pair], expert)
        return jnp.dot(hidden, w_down[expert], preferred_element_type=jnp.float32).astype(jnp.bfloat16)

    routed_all = lax.map(forward, pair_ids).reshape(pairs * per_pair, D)
    routed_out = routed_all[place].reshape(TOKENS, TOPW, D).astype(jnp.float32)
    mixed = jnp.sum(gates[:, :, None] * routed_out, axis=1)
    by_device = tokens.reshape(pairs, TOK_DEV, D)

    def local(device_id):
        expert = device_id % EXPERTS
        hidden = expert_hidden(by_device[device_id], expert)
        return jnp.dot(hidden, w_down[expert], preferred_element_type=jnp.float32)

    keep_f = keep.astype(jnp.float32)[:, None]
    local_out = keep_f * lax.map(local, pair_ids).reshape(TOKENS, D)
    difference = mixed - local_out
    upstream = cotangent.astype(jnp.float32) + difference
    routed_cot = (gates[:, :, None] * upstream[:, None, :]).astype(jnp.bfloat16).reshape(-1, D)
    local_cot = (-(keep_f * difference)).astype(jnp.bfloat16).reshape(pairs, TOK_DEV, D)
    cot_buffer = jnp.zeros((pairs * per_pair, D), routed_cot.dtype).at[place].set(routed_cot).reshape(pairs, per_pair, D)

    def backward(carry, group_id):
        def one_expert(expert):
            pair = group_id * EXPERTS + expert
            rows_x = jnp.concatenate([buffer[pair], by_device[pair]], axis=0)
            rows_c = jnp.concatenate([cot_buffer[pair], local_cot[pair]], axis=0)
            gate_act = jnp.dot(rows_x, w_gate[expert], preferred_element_type=jnp.float32)
            up_act = jnp.dot(rows_x, w_up[expert], preferred_element_type=jnp.float32)
            silu_val, slope = logistic_parts(gate_act)
            hidden = (silu_val * up_act).astype(jnp.bfloat16)
            grad_hidden = dot_back(rows_c, w_down[expert])
            gate_back = (grad_hidden * up_act * slope).astype(jnp.bfloat16)
            up_back = (grad_hidden * silu_val).astype(jnp.bfloat16)
            back_rows = dot_back(gate_back, w_gate[expert]) + dot_back(up_back, w_up[expert])
            grads = jnp.concatenate([dot_rows(rows_x, gate_back), dot_rows(rows_x, up_back), dot_rows(rows_c, hidden)], axis=1)
            return back_rows[:per_pair].astype(jnp.bfloat16), back_rows[per_pair:], grads

        routed_back, local_back, grads = lax.map(one_expert, jnp.arange(EXPERTS, dtype=jnp.int32))
        return carry + grads, (routed_back, local_back)

    start = jnp.zeros((EXPERTS, D, 3 * FF), jnp.float32)
    total, outputs = lax.scan(backward, start, jnp.arange(N_DP, dtype=jnp.int32))
    routed_back, local_back = outputs
    picked = routed_back.reshape(pairs * per_pair, D)[place].reshape(TOKENS, TOPW, D).astype(jnp.float32)
    token_grads = (jnp.sum(picked, axis=1) + local_back.reshape(TOKENS, D)).astype(jnp.bfloat16)
    return (token_grads, total * (1.0 / N_DP))
```

```python
import jax
import jax.numpy as jnp
from jax import lax
from jax.experimental import pallas as pl
from jax.experimental.pallas import tpu as pltpu
from jax.sharding import PartitionSpec as P

MESH = pl.DeviceIdType.MESH
BF = jnp.bfloat16
F32 = jnp.float32
NQ = 4
SELF = 28


def dot(a, b):
    return jnp.dot(a, b, preferred_element_type=F32)


def dot_nt(a, b):
    return lax.dot_general(a, b, (((1,), (1,)), ((), ())), preferred_element_type=F32)


def dot_tn(a, b):
    return lax.dot_general(a, b, (((0,), (0,)), ((), ())), preferred_element_type=F32)


def onehot(mask):
    return jnp.where(mask, 1.0, 0.0).astype(BF)


def iota(shape, axis):
    return lax.broadcasted_iota(jnp.int32, shape, axis)


def loop(n, body):
    def step(i, carry):
        body(i)
        return carry

    lax.fori_loop(0, n, step, 0)


def kernel(
    aux_ref, tok_hbm, cot_hbm, wg_hbm, wu_hbm, wd_hbm,
    otok_hbm, ograd_hbm,
    xall, call, cot, wg, wu, wd, gacc, uacc, hid, gh, gb, ub, locb, tokout,
    lmat, dmat, umat, pmat, sa, ra, sb, rb,
    ownd, owng, s1d, s1g, r1d, r1g, r2d, r2g,
    ld_sem, st_sem, ssem, rsem, s1s, s1r, s2s, s2r,
):
    me = lax.axis_index("expert")
    dp = lax.axis_index("dp")
    z, y = me // 4, me % 4
    xx, core = dp // 2, dp % 2

    def chunk(i):
        return (xx + 1 + i) % 4

    def load(part, q):
        cols = pl.ds(pl.multiple_of(q * 512, 512), 512)
        src, dst = (
            (tok_hbm.at[:, cols], xall.at[q, pl.ds(384, 128)]),
            (wg_hbm.at[cols], wg.at[q]),
            (wu_hbm.at[cols], wu.at[q]),
            (wd_hbm.at[:, cols], wd.at[q]),
            (cot_hbm.at[:, cols], cot.at[q]),
        )[part]
        return pltpu.make_async_copy(src, dst, ld_sem.at[part, q])

    for part in range(5):
        for i in range(NQ):
            load(part, chunk(i)).start()

    bar = pltpu.get_barrier_semaphore()
    for i in range(1, 32):
        pl.semaphore_signal(bar, inc=1, device_id={"expert": (me + i) % 32}, device_id_type=MESH)
    for i in range(1, 4):
        pl.semaphore_signal(bar, inc=1, device_id={"dp": ((xx + i) % 4) * 2 + core}, device_id_type=MESH)
    pl.semaphore_signal(bar, inc=1, device_id={"dp": xx * 2 + 1 - core}, device_id_type=MESH)

    aux = aux_ref[...]
    lanes = iota((128, 128), 1)
    subs = iota((128, 128), 0)
    eye = lanes == subs
    experts = [aux[:, k : k + 1].astype(jnp.int32) for k in range(2)]
    hots = [onehot(lanes == e) for e in experts]
    before = dot(onehot(lanes < subs), hots[0] + hots[1])
    for k in range(2):
        e = experts[k]
        s = jnp.sum(before * hots[k].astype(F32), axis=1, keepdims=True).astype(jnp.int32)
        dz = ((e >> 2) - z) & 7
        dy = ((e & 3) - y) & 3
        base = (((3 * dz + 7) & 7) * 4 + dy) * 16
        targets = [base + s]
        for j in range(3):
            targets.append(jnp.where((s >> 2) == j, base + 12 + (s & 3), -1))
        rows = []
        for t in range(4):
            dmat[t, pl.ds(128 * k, 128), :] = onehot(iota((128, 512), 1) == targets[t])
            spread = jnp.where(eye, targets[t].astype(F32), 0.0)
            rows.append(jnp.sum(spread, axis=0, keepdims=True).astype(jnp.int32))
        for j in range(3):
            lmat[j, :, pl.ds(256 * k, 128)] = onehot(iota((512, 128), 0) == rows[0])
            lmat[j, :, pl.ds(256 * k + 128, 128)] = onehot(iota((512, 128), 0) == rows[1 + j])

    def exchange(src, dst, a, q, sign):
        for p in range(32):
            m, dy = p // 4, p % 4
            dz = (3 * m + 3) % 8
            block = pl.ds(16 * p, 16)
            if p == SELF:
                pltpu.make_async_copy(src.at[q, block], dst.at[q, block], rsem.at[a, q]).start()
            else:
                to = ((z + sign * dz + 8) % 8) * 4 + (y + sign * dy + 4) % 4
                pltpu.make_async_remote_copy(
                    src_ref=src.at[q, block], dst_ref=dst.at[q, block],
                    send_sem=ssem.at[a, q], recv_sem=rsem.at[a, q],
                    device_id={"expert": to}, device_id_type=MESH,
                ).start()

    def arrived(dst, a, q):
        pltpu.make_async_copy(dst.at[q], dst.at[q], rsem.at[a, q]).wait()

    def sent(src, a, q):
        part = src.at[q, pl.ds(0, 496)]
        pltpu.make_async_copy(part, part, ssem.at[a, q]).wait()

    def scatter(dst, q, first, second):
        for j in range(3):
            part = slice(128 * j, 128 * j + 128)
            stack = jnp.concatenate(
                [first[:, part], first[:, 384:], second[:, part], second[:, 384:]], axis=0
            )
            dst[q, :, part] = dot(lmat[j], stack).astype(BF)

    def gather(mat, src, q):
        main = dot(mat[0], src[q])
        last = dot(mat[1], src[q, :, 0:128])
        last += dot(mat[2], src[q, :, 128:256])
        last += dot(mat[3], src[q, :, 256:384])
        return main, last

    pl.semaphore_wait(bar, 35)

    def dispatch(i):
        q = chunk(i)
        load(0, q).wait()
        rows = xall[q, 384:512, :]
        scatter(sa, q, rows, rows)
        exchange(sa, ra, 0, q, 1)

    loop(NQ, dispatch)

    row = iota((384, 512), 0)
    col = iota((384, 512), 1)
    blk = (row * 43691) >> 19
    s = row - 12 * blk
    umat[0] = onehot(col == 16 * blk + s)
    for j in range(3):
        umat[1 + j] = onehot((col == 16 * blk + 12 + (s & 3)) & ((s >> 2) == j))
    row = iota((512, 384), 0)
    col = iota((512, 384), 1)
    s = row & 15
    pmat[0] = onehot((s < 12) & (col == 12 * (row >> 4) + s))
    for j in range(3):
        pmat[1 + j] = onehot((s >= 12) & (col == 12 * (row >> 4) + 4 * j + s - 12))

    def pack(dst, q, main, last):
        for j in range(3):
            part = slice(128 * j, 128 * j + 128)
            dst[q, :, part] = (dot(pmat[0], main[:, part]) + dot(pmat[1 + j], last)).astype(BF)

    gacc[...] = jnp.zeros_like(gacc)
    uacc[...] = jnp.zeros_like(uacc)

    def forward_in(i):
        q = chunk(i)
        load(1, q).wait()
        load(2, q).wait()
        arrived(ra, 0, q)
        main, last = gather(umat, ra, q)
        xall[q, 0:384, 0:384] = main.astype(BF)
        xall[q, 0:384, 384:512] = last.astype(BF)
        gacc[...] += dot(xall[q], wg[q])
        uacc[...] += dot(xall[q], wu[q])

    loop(NQ, forward_in)

    def activate(r):
        rows = pl.ds(pl.multiple_of(r * 64, 64), 64)
        act = gacc[rows, :]
        hid[rows, :] = (act * jax.nn.sigmoid(act) * uacc[rows, :]).astype(BF)

    loop(8, activate)

    def forward_out(i):
        q = chunk(i)
        load(3, q).wait()
        result = dot(hid[0:384, :], wd[q]).astype(BF)
        pack(sb, q, result[:, 0:384], result[:, 384:512])
        exchange(sb, rb, 1, q, -1)

    loop(NQ, forward_out)

    gates = [aux[:, 2 + k : 3 + k] for k in range(2)]
    keep = aux[:, 4:5]

    def turn(i):
        q = chunk(i)
        load(4, q).wait()
        local = keep * dot(hid[384:512, :], wd[q])
        sent(sa, 0, q)
        arrived(rb, 1, q)
        main, last = gather(dmat, rb, q)
        picked = jnp.concatenate([main, last], axis=1)
        mixed = gates[0] * picked[0:128] + gates[1] * picked[128:256]
        difference = mixed - local
        upstream = cot[q].astype(F32) + difference
        scatter(sa, q, (gates[0] * upstream).astype(BF), (gates[1] * upstream).astype(BF))
        exchange(sa, ra, 2, q, 1)
        call[q, 384:512, :] = (-(keep * difference)).astype(BF)

    loop(NQ, turn)

    gh[...] = jnp.zeros_like(gh)
    mine = pl.ds(pl.multiple_of(core * 256, 256), 256)
    other = pl.ds(pl.multiple_of((1 - core) * 256, 256), 256)

    def to_core(src, dst, part, q):
        return pltpu.make_async_remote_copy(
            src_ref=src.at[q], dst_ref=dst.at[q], send_sem=s1s.at[part, q], recv_sem=s1r.at[part, q],
            device_id={"dp": xx * 2 + 1 - core}, device_id_type=MESH,
        )

    def to_chip(src, dst, part, i):
        return pltpu.make_async_remote_copy(
            src_ref=src.at[chunk(i)], dst_ref=dst.at[2 - i],
            send_sem=s2s.at[part, i], recv_sem=s2r.at[part, 2 - i],
            device_id={"dp": chunk(i) * 2 + core}, device_id_type=MESH,
        )

    def backward_in(i):
        q = chunk(i)
        arrived(ra, 2, q)
        main, last = gather(umat, ra, q)
        call[q, 0:384, 0:384] = main.astype(BF)
        call[q, 0:384, 384:512] = last.astype(BF)
        gh[...] += dot_nt(call[q], wd[q])
        s1d[q] = dot_tn(call[q, :, other], hid[...]).astype(BF)
        to_core(s1d, r1d, 0, q).start()
        ownd[q] = dot_tn(call[q, :, mine], hid[...])

    loop(NQ, backward_in)

    def activate_back(r):
        rows = pl.ds(pl.multiple_of(r * 64, 64), 64)
        act = gacc[rows, :]
        grad = gh[rows, :]
        sigma = jax.nn.sigmoid(act)
        gb[rows, :] = (grad * uacc[rows, :] * (sigma * (1.0 + act * (1.0 - sigma)))).astype(BF)
        ub[rows, :] = (grad * (act * sigma)).astype(BF)

    loop(8, activate_back)

    def backward_out(i):
        q = chunk(i)
        sent(sb, 1, q)
        back = dot_nt(gb[...], wg[q]) + dot_nt(ub[...], wu[q])
        routed = back[0:384].astype(BF)
        pack(sb, q, routed[:, 0:384], routed[:, 384:512])
        exchange(sb, rb, 3, q, -1)
        locb[q] = back[384:512]

    loop(NQ, backward_out)

    def pass_on(own, recv, dst, part, i):
        q = chunk(i)
        to_core(recv, recv, part, q).wait_recv()
        recv[q] = (own[q] + recv[q].astype(F32)).astype(BF)
        to_chip(recv, dst, part, i).start()

    loop(3, lambda i: pass_on(ownd, r1d, r2d, 0, i))

    def weight_grads(i):
        q = chunk(i)
        away = xall[q, :, other]
        s1g[q, :, 0:768] = dot_tn(away, gb[...]).astype(BF)
        s1g[q, :, 768:1536] = dot_tn(away, ub[...]).astype(BF)
        to_core(s1g, r1g, 1, q).start()
        here = xall[q, :, mine]
        owng[q, :, 0:768] = dot_tn(here, gb[...])
        owng[q, :, 768:1536] = dot_tn(here, ub[...])

        @pl.when(i > 0)
        def _():
            pass_on(owng, r1g, r2g, 1, i - 1)

    loop(NQ, weight_grads)

    def finish(i):
        q = chunk(i)
        arrived(rb, 3, q)
        main, last = gather(dmat, rb, q)
        picked = jnp.concatenate([main, last], axis=1)
        tokout[q] = (picked[0:128] + picked[128:256] + locb[q]).astype(BF)
        cols = pl.ds(pl.multiple_of(q * 512, 512), 512)
        pltpu.make_async_copy(tokout.at[q], otok_hbm.at[:, cols], st_sem.at[q]).start()

    loop(NQ, finish)

    def total(own, recv, got, part):
        to_core(recv, recv, part, xx).wait_recv()
        own[xx] = own[xx] + recv[xx].astype(F32)
        for i in range(3):
            to_chip(recv, got, part, i).wait_recv()
        own[xx] = (own[xx] + got[0].astype(F32) + got[1].astype(F32) + got[2].astype(F32)) * 0.125

    total(ownd, r1d, r2d, 0)
    out_d = pltpu.make_async_copy(ownd.at[xx], ograd_hbm.at[:, pl.ds(1536, 768)], st_sem.at[4])
    out_d.start()
    total(owng, r1g, r2g, 1)
    out_g = pltpu.make_async_copy(owng.at[xx], ograd_hbm.at[:, pl.ds(0, 1536)], st_sem.at[5])
    out_g.start()

    def drain(i):
        q = chunk(i)
        sent(sa, 2, q)
        sent(sb, 3, q)
        to_core(s1d, r1d, 0, q).wait_send()
        to_core(s1g, r1g, 1, q).wait_send()
        cols = pl.ds(pl.multiple_of(q * 512, 512), 512)
        pltpu.make_async_copy(tokout.at[q], otok_hbm.at[:, cols], st_sem.at[q]).wait()

    loop(NQ, drain)
    for i in range(3):
        to_chip(r1d, r2d, 0, i).wait_send()
        to_chip(r1g, r2g, 1, i).wait_send()
    out_d.wait()
    out_g.wait()


def on_device(tokens, routes, gates, keep, cotangent, w_gate, w_up, w_down):
    aux = jnp.concatenate(
        [routes.astype(F32), gates, keep.astype(F32)[:, None]], axis=1
    )
    hbm = pl.BlockSpec(memory_space=pl.ANY)
    vmem = pl.BlockSpec(memory_space=pltpu.VMEM)
    sem = pltpu.SemaphoreType.DMA
    token_grads, expert_grads = pl.pallas_call(
        kernel,
        out_shape=(
            jax.ShapeDtypeStruct((128, 2048), BF),
            jax.ShapeDtypeStruct((256, 2304), F32),
        ),
        in_specs=[vmem] + [hbm] * 5,
        out_specs=(hbm, hbm),
        scratch_shapes=[
            pltpu.VMEM((4, 512, 512), BF),
            pltpu.VMEM((4, 512, 512), BF),
            pltpu.VMEM((4, 128, 512), BF),
            pltpu.VMEM((4, 512, 768), BF),
            pltpu.VMEM((4, 512, 768), BF),
            pltpu.VMEM((4, 768, 512), BF),
            pltpu.VMEM((512, 768), F32),
            pltpu.VMEM((512, 768), F32),
            pltpu.VMEM((512, 768), BF),
            pltpu.VMEM((512, 768), F32),
            pltpu.VMEM((512, 768), BF),
            pltpu.VMEM((512, 768), BF),
            pltpu.VMEM((4, 128, 512), F32),
            pltpu.VMEM((4, 128, 512), BF),
            pltpu.VMEM((3, 512, 512), BF),
            pltpu.VMEM((4, 256, 512), BF),
            pltpu.VMEM((4, 384, 512), BF),
            pltpu.VMEM((4, 512, 384), BF),
            pltpu.VMEM((4, 512, 384), BF),
            pltpu.VMEM((4, 512, 384), BF),
            pltpu.VMEM((4, 512, 384), BF),
            pltpu.VMEM((4, 512, 384), BF),
            pltpu.VMEM((4, 256, 768), F32),
            pltpu.VMEM((4, 256, 1536), F32),
            pltpu.VMEM((4, 256, 768), BF),
            pltpu.VMEM((4, 256, 1536), BF),
            pltpu.VMEM((4, 256, 768), BF),
            pltpu.VMEM((4, 256, 1536), BF),
            pltpu.VMEM((3, 256, 768), BF),
            pltpu.VMEM((3, 256, 1536), BF),
            sem((5, 4)), sem((6,)), sem((4, 4)), sem((4, 4)),
            sem((2, 4)), sem((2, 4)), sem((2, 3)), sem((2, 3)),
        ],
        compiler_params=pltpu.CompilerParams(
            collective_id=0, has_side_effects=True, vmem_limit_bytes=67043328
        ),
    )(aux, tokens, cotangent, w_gate[0], w_up[0], w_down[0])
    return token_grads, expert_grads[None]


def solution(mesh):
    return jax.shard_map(
        on_device,
        mesh=mesh,
        in_specs=(
            P(("dp", "expert"), None),
            P(("dp", "expert"), None),
            P(("dp", "expert"), None),
            P(("dp", "expert")),
            P(("dp", "expert"), None),
            P("expert", None, None),
            P("expert", None, None),
            P("expert", None, None),
        ),
        out_specs=(P(("dp", "expert"), None), P("expert", "dp", None)),
        check_vma=False,
    )
```

```python
import functools

import jax
import jax.numpy as jnp
from jax import lax
from jax.experimental import pallas as pl
from jax.experimental.pallas import tpu as pltpu
from jax.sharding import PartitionSpec as P

MESH = pl.DeviceIdType.MESH
BF = jnp.bfloat16
F32 = jnp.float32
NQ = 4
ORDER = (1, 7, 3, 5, 2, 6, 4, 0)
SELF = 28


def dot(a, b):
    return jnp.dot(a, b, preferred_element_type=F32)


def dot_nt(a, b):
    return lax.dot_general(a, b, (((1,), (1,)), ((), ())), preferred_element_type=F32)


def dot_tn(a, b):
    return lax.dot_general(a, b, (((0,), (0,)), ((), ())), preferred_element_type=F32)


def onehot(mask):
    return jnp.where(mask, 1.0, 0.0).astype(BF)


def iota(shape, axis):
    return lax.broadcasted_iota(jnp.int32, shape, axis)


def loop(n, body):
    def step(i, carry):
        body(i)
        return carry

    lax.fori_loop(0, n, step, 0)


def kernel(
    routes_ref, gates_ref, keep_ref, tok_hbm, cot_hbm, wg_hbm, wu_hbm, wd_hbm,
    otok_hbm, ograd_hbm,
    xall, call, cot, wg, wu, wd, gacc, uacc, hid, gh, gb, ub, locb, tokout,
    lmat, dmat, umat, pmat, sa, ra, sb, rb,
    ownd, owng, s1d, s1g, r1d, r1g, r2d, r2g, hd, hg,
    ld_sem, st_sem, ssem, rsem, s1s, s1r, s2s, s2r,
):
    me = lax.axis_index("expert")
    dp = lax.axis_index("dp")
    z, y = me // 4, me % 4
    xx, core = dp // 2, dp % 2

    def chunk(i):
        if isinstance(i, int):
            return (xx + (2, 1, 3, 0)[i]) % 4
        return (xx + jnp.where(i == 0, 2, jnp.where(i == 3, 0, 2 * i - 1))) % 4

    def load(part, q):
        cols = pl.ds(pl.multiple_of(q * 512, 512), 512)
        src, dst = (
            (tok_hbm.at[:, cols], xall.at[q, pl.ds(384, 128)]),
            (wg_hbm.at[cols], wg.at[q]),
            (wu_hbm.at[cols], wu.at[q]),
            (wd_hbm.at[:, cols], wd.at[q]),
            (cot_hbm.at[:, cols], cot.at[q]),
        )[part]
        return pltpu.make_async_copy(src, dst, ld_sem.at[part, q])

    for part in range(5):
        for i in range(NQ):
            load(part, chunk(i)).start()

    bar = pltpu.get_barrier_semaphore()
    for i in range(1, 32):
        pl.semaphore_signal(bar, inc=1, device_id={"expert": (me + i) % 32}, device_id_type=MESH)
    for i in range(1, 4):
        pl.semaphore_signal(bar, inc=1, device_id={"dp": ((xx + i) % 4) * 2 + core}, device_id_type=MESH)
    pl.semaphore_signal(bar, inc=1, device_id={"dp": xx * 2 + 1 - core}, device_id_type=MESH)

    lanes = iota((128, 128), 1)
    subs = iota((128, 128), 0)
    eye = lanes == subs

    def column(row):
        return jnp.sum(jnp.where(eye, row, jnp.zeros_like(row)), axis=1, keepdims=True)

    experts = [column(routes_ref[k : k + 1, :].astype(F32)).astype(jnp.int32) for k in range(2)]
    hots = [onehot(lanes == e) for e in experts]
    before = dot(onehot(lanes < subs), hots[0] + hots[1])
    for k in range(2):
        e = experts[k]
        s = jnp.sum(before * hots[k].astype(F32), axis=1, keepdims=True).astype(jnp.int32)
        dz = ((e >> 2) - z) & 7
        dy = ((e & 3) - y) & 3
        turn_of = sum(jnp.where(dz == d, m, 0) for m, d in enumerate(ORDER))
        base = (turn_of * 4 + dy) * 16
        targets = [base + s]
        for j in range(3):
            targets.append(jnp.where((s >> 2) == j, base + 12 + (s & 3), -1))
        rows = []
        for t in range(4):
            dmat[t, pl.ds(128 * k, 128), :] = onehot(iota((128, 512), 1) == targets[t])
            spread = jnp.where(eye, targets[t].astype(F32), 0.0)
            rows.append(jnp.sum(spread, axis=0, keepdims=True).astype(jnp.int32))
        for j in range(3):
            lmat[j, :, pl.ds(256 * k, 128)] = onehot(iota((512, 128), 0) == rows[0])
            lmat[j, :, pl.ds(256 * k + 128, 128)] = onehot(iota((512, 128), 0) == rows[1 + j])

    def exchange(src, dst, a, q, sign):
        for p in range(32):
            dz, dy = ORDER[p // 4], p % 4
            block = pl.ds(16 * p, 16)
            if p == SELF:
                pltpu.make_async_copy(src.at[q, block], dst.at[q, block], rsem.at[a, q]).start()
            else:
                to = ((z + sign * dz + 8) % 8) * 4 + (y + sign * dy + 4) % 4
                pltpu.make_async_remote_copy(
                    src_ref=src.at[q, block], dst_ref=dst.at[q, block],
                    send_sem=ssem.at[a, q], recv_sem=rsem.at[a, q],
                    device_id={"expert": to}, device_id_type=MESH,
                ).start()

    def arrived(dst, a, q):
        pltpu.make_async_copy(dst.at[q], dst.at[q], rsem.at[a, q]).wait()

    def sent(src, a, q):
        part = src.at[q, pl.ds(0, 496)]
        pltpu.make_async_copy(part, part, ssem.at[a, q]).wait()

    def scatter(dst, q, first, second):
        for j in range(3):
            part = slice(128 * j, 128 * j + 128)
            stack = jnp.concatenate(
                [first[:, part], first[:, 384:], second[:, part], second[:, 384:]], axis=0
            )
            dst[q, :, part] = dot(lmat[j], stack).astype(BF)

    def gather(mat, src, q):
        main = dot(mat[0], src[q])
        last = dot(mat[1], src[q, :, 0:128])
        last += dot(mat[2], src[q, :, 128:256])
        last += dot(mat[3], src[q, :, 256:384])
        return main, last

    def dispatch(i):
        q = chunk(i)
        load(0, q).wait()
        rows = xall[q, 384:512, :]
        scatter(sa, q, rows, rows)

    loop(NQ, dispatch)
    pl.semaphore_wait(bar, 35)
    loop(NQ, lambda i: exchange(sa, ra, 0, chunk(i), 1))

    row = iota((384, 512), 0)
    col = iota((384, 512), 1)
    blk = (row * 43691) >> 19
    s = row - 12 * blk
    umat[0] = onehot(col == 16 * blk + s)
    for j in range(3):
        umat[1 + j] = onehot((col == 16 * blk + 12 + (s & 3)) & ((s >> 2) == j))
    row = iota((512, 384), 0)
    col = iota((512, 384), 1)
    s = row & 15
    pmat[0] = onehot((s < 12) & (col == 12 * (row >> 4) + s))
    for j in range(3):
        pmat[1 + j] = onehot((s >= 12) & (col == 12 * (row >> 4) + 4 * j + s - 12))

    def pack(dst, q, main, last):
        for j in range(3):
            part = slice(128 * j, 128 * j + 128)
            dst[q, :, part] = (dot(pmat[0], main[:, part]) + dot(pmat[1 + j], last)).astype(BF)

    gacc[...] = jnp.zeros_like(gacc)
    uacc[...] = jnp.zeros_like(uacc)

    def forward_in(i):
        q = chunk(i)
        load(1, q).wait()
        load(2, q).wait()
        arrived(ra, 0, q)
        main, last = gather(umat, ra, q)
        xall[q, 0:384, 0:384] = main.astype(BF)
        xall[q, 0:384, 384:512] = last.astype(BF)
        gacc[...] += dot(xall[q], wg[q])
        uacc[...] += dot(xall[q], wu[q])

    loop(NQ, forward_in)

    def activate(r):
        rows = pl.ds(pl.multiple_of(r * 64, 64), 64)
        act = gacc[rows, :]
        hid[rows, :] = (act * jax.nn.sigmoid(act) * uacc[rows, :]).astype(BF)

    loop(8, activate)

    def forward_out(i):
        q = chunk(i)
        load(3, q).wait()
        result = dot(hid[0:384, :], wd[q]).astype(BF)
        pack(sb, q, result[:, 0:384], result[:, 384:512])
        exchange(sb, rb, 1, q, -1)

    loop(NQ, forward_out)

    def factors(r):
        rows = pl.ds(pl.multiple_of(r * 64, 64), 64)
        act = gacc[rows, :]
        sigma = jax.nn.sigmoid(act)
        gacc[rows, :] = uacc[rows, :] * (sigma * (1.0 + act * (1.0 - sigma)))
        uacc[rows, :] = act * sigma

    loop(8, factors)

    gates = [column(gates_ref[k : k + 1, :]) for k in range(2)]
    keep = column(keep_ref[...].astype(F32))

    def turn(i):
        q = chunk(i)
        load(4, q).wait()
        local = keep * dot(hid[384:512, :], wd[q])
        sent(sa, 0, q)
        arrived(rb, 1, q)
        main, last = gather(dmat, rb, q)
        picked = jnp.concatenate([main, last], axis=1)
        mixed = gates[0] * picked[0:128] + gates[1] * picked[128:256]
        difference = mixed - local
        upstream = cot[q].astype(F32) + difference
        scatter(sa, q, (gates[0] * upstream).astype(BF), (gates[1] * upstream).astype(BF))
        exchange(sa, ra, 2, q, 1)
        call[q, 384:512, :] = (-(keep * difference)).astype(BF)

    loop(NQ, turn)

    gh[...] = jnp.zeros_like(gh)
    mine = pl.ds(pl.multiple_of(core * 256, 256), 256)
    other = pl.ds(pl.multiple_of((1 - core) * 256, 256), 256)

    def to_core(src, dst, part, q):
        return pltpu.make_async_remote_copy(
            src_ref=src.at[q], dst_ref=dst.at[q], send_sem=s1s.at[part, q], recv_sem=s1r.at[part, q],
            device_id={"dp": xx * 2 + 1 - core}, device_id_type=MESH,
        )

    def to_chip(src, dst, part, n, dx):
        return pltpu.make_async_remote_copy(
            src_ref=src, dst_ref=dst, send_sem=s2s.at[part, n], recv_sem=s2r.at[part, n],
            device_id={"dp": ((xx + dx) % 4) * 2 + core}, device_id_type=MESH,
        )

    low, high = pl.ds(0, 128), pl.ds(128, 128)

    def hops(part, k):
        recv, half, got = ((r1d, hd, r2d), (r1g, hg, r2g))[part]
        block = recv.at[chunk(k)]
        if k == 0:
            return (
                to_chip(block.at[low], half.at[0], part, 0, 1),
                to_chip(block.at[high], half.at[1], part, 1, 3),
            )
        return (to_chip(block, got.at[k - 1], part, 1 + k, (1, 3)[k - 1]),)

    def pass_on(part, k):
        own, recv, half = ((ownd, r1d, hd), (owng, r1g, hg))[part]
        q = chunk(k)
        to_core(recv, recv, part, q).wait_recv()
        if k == 0:
            recv[q] = (own[q] + recv[q].astype(F32)).astype(BF)
        else:
            hops(part, 0)[k - 1].wait_recv()
            plain, added = ((high, low), (low, high))[k - 1]
            recv[q, plain] = (own[q, plain] + recv[q, plain].astype(F32)).astype(BF)
            recv[q, added] = (
                own[q, added] + recv[q, added].astype(F32) + half[k - 1].astype(F32)
            ).astype(BF)
        for hop in hops(part, k):
            hop.start()

    def down_grads(i):
        q = chunk(i)
        s1d[q] = dot_tn(call[q, :, other], hid[...]).astype(BF)
        to_core(s1d, r1d, 0, q).start()
        ownd[q] = dot_tn(call[q, :, mine], hid[...])

    def backward_in(i):
        q = chunk(i)
        arrived(ra, 2, q)
        main, last = gather(umat, ra, q)
        call[q, 0:384, 0:384] = main.astype(BF)
        call[q, 0:384, 384:512] = last.astype(BF)
        gh[...] += dot_nt(call[q], wd[q])

        @pl.when(i < 3)
        def _():
            down_grads(i)

        for k in range(2):
            pl.when(i == k + 1)(functools.partial(pass_on, 0, k))

    loop(NQ, backward_in)

    def activate_back(r):
        rows = pl.ds(pl.multiple_of(r * 64, 64), 64)
        grad = gh[rows, :]
        gb[rows, :] = (grad * gacc[rows, :]).astype(BF)
        ub[rows, :] = (grad * uacc[rows, :]).astype(BF)

    loop(8, activate_back)

    def backward_out(i):
        q = chunk(i)
        sent(sb, 1, q)
        routed = (dot_nt(gb[0:384, :], wg[q]) + dot_nt(ub[0:384, :], wu[q])).astype(BF)
        pack(sb, q, routed[:, 0:384], routed[:, 384:512])
        exchange(sb, rb, 3, q, -1)

        @pl.when(i == 0)
        def _():
            pass_on(0, 2)

        away = xall[q, :, other]
        s1g[q, :, 0:768] = dot_tn(away, gb[...]).astype(BF)
        s1g[q, :, 768:1536] = dot_tn(away, ub[...]).astype(BF)
        to_core(s1g, r1g, 1, q).start()
        here = xall[q, :, mine]
        owng[q, :, 0:768] = dot_tn(here, gb[...])
        owng[q, :, 768:1536] = dot_tn(here, ub[...])

        @pl.when(i == 0)
        def _():
            down_grads(3)

        for k in range(3):
            pl.when(i == k + 1)(functools.partial(pass_on, 1, k))
        locb[q] = dot_nt(gb[384:512, :], wg[q]) + dot_nt(ub[384:512, :], wu[q])

    loop(NQ, backward_out)

    def total(part):
        own, recv, got = ((ownd, r1d, r2d), (owng, r1g, r2g))[part]
        to_core(recv, recv, part, xx).wait_recv()
        own[xx] = own[xx] + recv[xx].astype(F32)
        hops(part, 1)[0].wait_recv()
        hops(part, 2)[0].wait_recv()
        own[xx] = (own[xx] + got[0].astype(F32) + got[1].astype(F32)) * 0.125
        width = 768 * (1 + part)
        copy = pltpu.make_async_copy(
            own.at[xx], ograd_hbm.at[:, pl.ds(1536 * (1 - part), width)], st_sem.at[4 + part]
        )
        copy.start()
        return copy

    def finish(i):
        q = chunk(i)
        arrived(rb, 3, q)
        main, last = gather(dmat, rb, q)
        picked = jnp.concatenate([main, last], axis=1)
        tokout[q] = (picked[0:128] + picked[128:256] + locb[q]).astype(BF)
        cols = pl.ds(pl.multiple_of(q * 512, 512), 512)
        pltpu.make_async_copy(tokout.at[q], otok_hbm.at[:, cols], st_sem.at[q]).start()

    out_d = total(0)
    loop(3, finish)
    out_g = total(1)
    finish(3)

    def drain(i):
        q = chunk(i)
        sent(sa, 2, q)
        sent(sb, 3, q)
        to_core(s1d, r1d, 0, q).wait_send()
        to_core(s1g, r1g, 1, q).wait_send()
        cols = pl.ds(pl.multiple_of(q * 512, 512), 512)
        pltpu.make_async_copy(tokout.at[q], otok_hbm.at[:, cols], st_sem.at[q]).wait()

    loop(NQ, drain)
    for part in range(2):
        for k in range(3):
            for hop in hops(part, k):
                hop.wait_send()
    out_d.wait()
    out_g.wait()


def on_device(tokens, routes, gates, keep, cotangent, w_gate, w_up, w_down):
    hbm = pl.BlockSpec(memory_space=pl.ANY)
    vmem = pl.BlockSpec(memory_space=pltpu.VMEM)
    sem = pltpu.SemaphoreType.DMA
    token_grads, expert_grads = pl.pallas_call(
        kernel,
        out_shape=(
            jax.ShapeDtypeStruct((128, 2048), BF),
            jax.ShapeDtypeStruct((256, 2304), F32),
        ),
        in_specs=[vmem] * 3 + [hbm] * 5,
        out_specs=(hbm, hbm),
        scratch_shapes=[
            pltpu.VMEM((4, 512, 512), BF),
            pltpu.VMEM((4, 512, 512), BF),
            pltpu.VMEM((4, 128, 512), BF),
            pltpu.VMEM((4, 512, 768), BF),
            pltpu.VMEM((4, 512, 768), BF),
            pltpu.VMEM((4, 768, 512), BF),
            pltpu.VMEM((512, 768), F32),
            pltpu.VMEM((512, 768), F32),
            pltpu.VMEM((512, 768), BF),
            pltpu.VMEM((512, 768), F32),
            pltpu.VMEM((512, 768), BF),
            pltpu.VMEM((512, 768), BF),
            pltpu.VMEM((4, 128, 512), F32),
            pltpu.VMEM((4, 128, 512), BF),
            pltpu.VMEM((3, 512, 512), BF),
            pltpu.VMEM((4, 256, 512), BF),
            pltpu.VMEM((4, 384, 512), BF),
            pltpu.VMEM((4, 512, 384), BF),
            pltpu.VMEM((4, 512, 384), BF),
            pltpu.VMEM((4, 512, 384), BF),
            pltpu.VMEM((4, 512, 384), BF),
            pltpu.VMEM((4, 512, 384), BF),
            pltpu.VMEM((4, 256, 768), F32),
            pltpu.VMEM((4, 256, 1536), F32),
            pltpu.VMEM((4, 256, 768), BF),
            pltpu.VMEM((4, 256, 1536), BF),
            pltpu.VMEM((4, 256, 768), BF),
            pltpu.VMEM((4, 256, 1536), BF),
            pltpu.VMEM((2, 256, 768), BF),
            pltpu.VMEM((2, 256, 1536), BF),
            pltpu.VMEM((2, 128, 768), BF),
            pltpu.VMEM((2, 128, 1536), BF),
            sem((5, 4)), sem((6,)), sem((4, 4)), sem((4, 4)),
            sem((2, 4)), sem((2, 4)), sem((2, 4)), sem((2, 4)),
        ],
        compiler_params=pltpu.CompilerParams(
            collective_id=0, has_side_effects=True, vmem_limit_bytes=67043328
        ),
    )(routes.T, gates.T, keep.reshape(1, 128), tokens, cotangent, w_gate[0], w_up[0], w_down[0])
    return token_grads, expert_grads[None]


def solution(mesh):
    return jax.shard_map(
        on_device,
        mesh=mesh,
        in_specs=(
            P(("dp", "expert"), None),
            P(("dp", "expert"), None),
            P(("dp", "expert"), None),
            P(("dp", "expert")),
            P(("dp", "expert"), None),
            P("expert", None, None),
            P("expert", None, None),
            P("expert", None, None),
        ),
        out_specs=(P(("dp", "expert"), None), P("expert", "dp", None)),
        check_vma=False,
    )
```

```python
import functools

import jax
import jax.numpy as jnp
from jax import lax
from jax.experimental import pallas as pl
from jax.experimental.pallas import tpu as pltpu
from jax.sharding import PartitionSpec as P

MESH = pl.DeviceIdType.MESH
BF = jnp.bfloat16
F32 = jnp.float32
NQ = 4
ORDER = (1, 7, 3, 5, 2, 6, 4, 0)
SELF = 28


def dot(a, b):
    return jnp.dot(a, b, preferred_element_type=F32)


def dot_nt(a, b):
    return lax.dot_general(a, b, (((1,), (1,)), ((), ())), preferred_element_type=F32)


def dot_tn(a, b):
    return lax.dot_general(a, b, (((0,), (0,)), ((), ())), preferred_element_type=F32)


def onehot(mask):
    return jnp.where(mask, 1.0, 0.0).astype(BF)


def pair(g):
    return pl.ds(256 * g, 256), pl.ds(192 * g, 192)


def iota(shape, axis):
    return lax.broadcasted_iota(jnp.int32, shape, axis)


def loop(n, body):
    def step(i, carry):
        body(i)
        return carry

    lax.fori_loop(0, n, step, 0)


def kernel(
    routes_ref, gates_ref, keep_ref, tok_hbm, cot_hbm, wg_hbm, wu_hbm, wd_hbm,
    otok, ograd,
    xall, call, cot, wg, wu, wd, gacc, uacc, hid, gh, gb, ub, locb,
    lmat, dmat, umat, pmat, sa, ra, sb, rb,
    ownd, owng, s1d, s1g, r1d, r1g, r2d, r2g, hd, hg,
    ld_sem, ssem, rsem, s1s, s1r, s2s, s2r,
):
    me = lax.axis_index("expert")
    dp = lax.axis_index("dp")
    z, y = me // 4, me % 4
    xx, core = dp // 2, dp % 2

    def chunk(i):
        if isinstance(i, int):
            return (xx + (2, 1, 3, 0)[i]) % 4
        return (xx + jnp.where(i == 0, 2, jnp.where(i == 3, 0, 2 * i - 1))) % 4

    def load(part, q):
        cols = pl.ds(pl.multiple_of(q * 512, 512), 512)
        src, dst = (
            (tok_hbm.at[:, cols], xall.at[q, pl.ds(384, 128)]),
            (wg_hbm.at[cols], wg.at[q]),
            (wu_hbm.at[cols], wu.at[q]),
            (wd_hbm.at[:, cols], wd.at[q]),
            (cot_hbm.at[:, cols], cot.at[q]),
        )[part]
        return pltpu.make_async_copy(src, dst, ld_sem.at[part, q])

    for part in range(5):
        for i in range(NQ):
            load(part, chunk(i)).start()

    bar = pltpu.get_barrier_semaphore()
    for i in range(1, 32):
        pl.semaphore_signal(bar, inc=1, device_id={"expert": (me + i) % 32}, device_id_type=MESH)
    for i in range(1, 4):
        pl.semaphore_signal(bar, inc=1, device_id={"dp": ((xx + i) % 4) * 2 + core}, device_id_type=MESH)
    pl.semaphore_signal(bar, inc=1, device_id={"dp": xx * 2 + 1 - core}, device_id_type=MESH)

    lanes = iota((128, 128), 1)
    subs = iota((128, 128), 0)
    eye = lanes == subs

    def column(row):
        return jnp.sum(jnp.where(eye, row, jnp.zeros_like(row)), axis=1, keepdims=True)

    experts = [column(routes_ref[k : k + 1, :].astype(F32)).astype(jnp.int32) for k in range(2)]
    hots = [onehot(lanes == e) for e in experts]
    before = dot(onehot(lanes < subs), hots[0] + hots[1])
    for k in range(2):
        e = experts[k]
        s = jnp.sum(before * hots[k].astype(F32), axis=1, keepdims=True).astype(jnp.int32)
        dz = ((e >> 2) - z) & 7
        dy = ((e & 3) - y) & 3
        turn_of = sum(jnp.where(dz == d, m, 0) for m, d in enumerate(ORDER))
        base = (turn_of * 4 + dy) * 16
        targets = [base + s]
        for j in range(3):
            targets.append(jnp.where((s >> 2) == j, base + 12 + (s & 3), -1))
        rows = []
        for t in range(4):
            dmat[t, pl.ds(128 * k, 128), :] = onehot(iota((128, 512), 1) == targets[t])
            spread = jnp.where(eye, targets[t].astype(F32), 0.0)
            rows.append(jnp.sum(spread, axis=0, keepdims=True).astype(jnp.int32))
        for j in range(3):
            lmat[j, :, pl.ds(256 * k, 128)] = onehot(iota((512, 128), 0) == rows[0])
            lmat[j, :, pl.ds(256 * k + 128, 128)] = onehot(iota((512, 128), 0) == rows[1 + j])

    def exchange(src, dst, a, q, g, sign):
        for p in range(16 * g, 16 * g + 16):
            dz, dy = ORDER[p // 4], p % 4
            block = pl.ds(16 * p, 16)
            if p == SELF:
                pltpu.make_async_copy(src.at[q, block], dst.at[q, block], rsem.at[a, q, g]).start()
            else:
                to = ((z + sign * dz + 8) % 8) * 4 + (y + sign * dy + 4) % 4
                pltpu.make_async_remote_copy(
                    src_ref=src.at[q, block], dst_ref=dst.at[q, block],
                    send_sem=ssem.at[a, q], recv_sem=rsem.at[a, q, g],
                    device_id={"expert": to}, device_id_type=MESH,
                ).start()

    def exchange_all(src, dst, a, q, sign):
        exchange(src, dst, a, q, 0, sign)
        exchange(src, dst, a, q, 1, sign)

    def arrived(dst, a, q, g):
        part = dst.at[q, pair(g)[0]]
        pltpu.make_async_copy(part, part, rsem.at[a, q, g]).wait()

    def arrived_all(dst, a, q):
        arrived(dst, a, q, 0)
        arrived(dst, a, q, 1)

    def sent(src, a, q):
        part = src.at[q, pl.ds(0, 496)]
        pltpu.make_async_copy(part, part, ssem.at[a, q]).wait()

    def scatter(dst, q, first, second):
        for j in range(3):
            part = slice(128 * j, 128 * j + 128)
            stack = jnp.concatenate(
                [first[:, part], first[:, 384:], second[:, part], second[:, 384:]], axis=0
            )
            dst[q, :, part] = dot(lmat[j], stack).astype(BF)

    def gather(mat, src):
        main = dot(mat[0], src[...])
        last = dot(mat[1], src[:, 0:128])
        last += dot(mat[2], src[:, 128:256])
        last += dot(mat[3], src[:, 256:384])
        return main, last

    def unpack(dst, src, q, g):
        packed, plain = pair(g)
        main, last = gather(umat, src.at[q, packed])
        dst[q, plain, 0:384] = main.astype(BF)
        dst[q, plain, 384:512] = last.astype(BF)

    def dispatch(i):
        q = chunk(i)
        load(0, q).wait()
        rows = xall[q, 384:512, :]
        scatter(sa, q, rows, rows)

    loop(NQ, dispatch)
    pl.semaphore_wait(bar, 35)
    for g in range(2):
        loop(NQ, lambda i: exchange(sa, ra, 0, chunk(i), g, 1))

    row = iota((192, 256), 0)
    col = iota((192, 256), 1)
    blk = (row * 43691) >> 19
    s = row - 12 * blk
    umat[0] = onehot(col == 16 * blk + s)
    for j in range(3):
        umat[1 + j] = onehot((col == 16 * blk + 12 + (s & 3)) & ((s >> 2) == j))
    row = iota((256, 192), 0)
    col = iota((256, 192), 1)
    s = row & 15
    pmat[0] = onehot((s < 12) & (col == 12 * (row >> 4) + s))
    for j in range(3):
        pmat[1 + j] = onehot((s >= 12) & (col == 12 * (row >> 4) + 4 * j + s - 12))

    def pack(dst, q, g, rows):
        packed = pair(g)[0]
        for j in range(3):
            part = slice(128 * j, 128 * j + 128)
            dst[q, packed, part] = (dot(pmat[0], rows[:, part]) + dot(pmat[1 + j], rows[:, 384:])).astype(BF)

    gacc[...] = jnp.zeros_like(gacc)
    uacc[...] = jnp.zeros_like(uacc)

    def project(q, rows):
        gacc[rows, :] += dot(xall[q, rows, :], wg[q])
        uacc[rows, :] += dot(xall[q, rows, :], wu[q])

    def activate(r):
        rows = pl.ds(pl.multiple_of(r * 64, 64), 64)
        act = gacc[rows, :]
        hid[rows, :] = (act * jax.nn.sigmoid(act) * uacc[rows, :]).astype(BF)

    def local_in(i):
        q = chunk(i)
        load(1, q).wait()
        load(2, q).wait()
        project(q, pl.ds(384, 128))

    loop(NQ, local_in)
    loop(2, lambda r: activate(r + 6))

    def group(g):
        plain = pair(g)[1]

        def forward_in(i):
            q = chunk(i)
            arrived(ra, 0, q, g)
            unpack(xall, ra, q, g)
            project(q, plain)

        def forward_out(i):
            q = chunk(i)
            if g == 0:
                load(3, q).wait()
            pack(sb, q, g, dot(hid[plain, :], wd[q]).astype(BF))
            exchange(sb, rb, 1, q, g, -1)

        loop(NQ, forward_in)
        loop(3, lambda r: activate(r + 3 * g))
        loop(NQ, forward_out)

    group(0)
    group(1)

    def factors(r):
        rows = pl.ds(pl.multiple_of(r * 64, 64), 64)
        act = gacc[rows, :]
        sigma = jax.nn.sigmoid(act)
        gacc[rows, :] = uacc[rows, :] * (sigma * (1.0 + act * (1.0 - sigma)))
        uacc[rows, :] = act * sigma

    loop(8, factors)

    gates = [column(gates_ref[k : k + 1, :]) for k in range(2)]
    keep = column(keep_ref[...].astype(F32))

    def turn(i):
        q = chunk(i)
        load(4, q).wait()
        local = keep * dot(hid[384:512, :], wd[q])
        sent(sa, 0, q)
        arrived_all(rb, 1, q)
        main, last = gather(dmat, rb.at[q])
        picked = jnp.concatenate([main, last], axis=1)
        mixed = gates[0] * picked[0:128] + gates[1] * picked[128:256]
        difference = mixed - local
        upstream = cot[q].astype(F32) + difference
        scatter(sa, q, (gates[0] * upstream).astype(BF), (gates[1] * upstream).astype(BF))
        exchange_all(sa, ra, 2, q, 1)
        call[q, 384:512, :] = (-(keep * difference)).astype(BF)

    loop(NQ, turn)

    gh[...] = jnp.zeros_like(gh)
    mine = pl.ds(pl.multiple_of(core * 256, 256), 256)
    other = pl.ds(pl.multiple_of((1 - core) * 256, 256), 256)

    def to_core(src, dst, part, q):
        return pltpu.make_async_remote_copy(
            src_ref=src.at[q], dst_ref=dst.at[q], send_sem=s1s.at[part, q], recv_sem=s1r.at[part, q],
            device_id={"dp": xx * 2 + 1 - core}, device_id_type=MESH,
        )

    def to_chip(src, dst, part, n, dx):
        return pltpu.make_async_remote_copy(
            src_ref=src, dst_ref=dst, send_sem=s2s.at[part, n], recv_sem=s2r.at[part, n],
            device_id={"dp": ((xx + dx) % 4) * 2 + core}, device_id_type=MESH,
        )

    low, high = pl.ds(0, 128), pl.ds(128, 128)

    def hops(part, k):
        recv, half, got = ((r1d, hd, r2d), (r1g, hg, r2g))[part]
        block = recv.at[chunk(k)]
        if k == 0:
            return (
                to_chip(block.at[low], half.at[0], part, 0, 1),
                to_chip(block.at[high], half.at[1], part, 1, 3),
            )
        return (to_chip(block, got.at[k - 1], part, 1 + k, (1, 3)[k - 1]),)

    def pass_on(part, k):
        own, recv, half = ((ownd, r1d, hd), (owng, r1g, hg))[part]
        q = chunk(k)
        to_core(recv, recv, part, q).wait_recv()
        if k == 0:
            recv[q] = (own[q] + recv[q].astype(F32)).astype(BF)
        else:
            hops(part, 0)[k - 1].wait_recv()
            plain, added = ((high, low), (low, high))[k - 1]
            recv[q, plain] = (own[q, plain] + recv[q, plain].astype(F32)).astype(BF)
            recv[q, added] = (
                own[q, added] + recv[q, added].astype(F32) + half[k - 1].astype(F32)
            ).astype(BF)
        for hop in hops(part, k):
            hop.start()

    def down_grads(i):
        q = chunk(i)
        s1d[q] = dot_tn(call[q, :, other], hid[...]).astype(BF)
        to_core(s1d, r1d, 0, q).start()
        ownd[q] = dot_tn(call[q, :, mine], hid[...])

    def backward_in(i):
        q = chunk(i)
        for g in range(2):
            arrived(ra, 2, q, g)
            unpack(call, ra, q, g)
        gh[...] += dot_nt(call[q], wd[q])

        @pl.when(i < 3)
        def _():
            down_grads(i)

        for k in range(2):
            pl.when(i == k + 1)(functools.partial(pass_on, 0, k))

    loop(NQ, backward_in)

    def activate_back(r):
        rows = pl.ds(pl.multiple_of(r * 64, 64), 64)
        grad = gh[rows, :]
        gb[rows, :] = (grad * gacc[rows, :]).astype(BF)
        ub[rows, :] = (grad * uacc[rows, :]).astype(BF)

    loop(8, activate_back)

    def backward_out(i):
        q = chunk(i)
        sent(sb, 1, q)
        for g in range(2):
            plain = pair(g)[1]
            pack(sb, q, g, (dot_nt(gb[plain, :], wg[q]) + dot_nt(ub[plain, :], wu[q])).astype(BF))
            exchange(sb, rb, 3, q, g, -1)

        @pl.when(i == 0)
        def _():
            pass_on(0, 2)

        away = xall[q, :, other]
        s1g[q, :, 0:768] = dot_tn(away, gb[...]).astype(BF)
        s1g[q, :, 768:1536] = dot_tn(away, ub[...]).astype(BF)
        to_core(s1g, r1g, 1, q).start()
        here = xall[q, :, mine]
        owng[q, :, 0:768] = dot_tn(here, gb[...])
        owng[q, :, 768:1536] = dot_tn(here, ub[...])

        @pl.when(i == 0)
        def _():
            down_grads(3)

        for k in range(3):
            pl.when(i == k + 1)(functools.partial(pass_on, 1, k))
        locb[q] = dot_nt(gb[384:512, :], wg[q]) + dot_nt(ub[384:512, :], wu[q])

    loop(NQ, backward_out)

    def total(part):
        own, recv, got = ((ownd, r1d, r2d), (owng, r1g, r2g))[part]
        to_core(recv, recv, part, xx).wait_recv()
        own[xx] = own[xx] + recv[xx].astype(F32)
        hops(part, 1)[0].wait_recv()
        hops(part, 2)[0].wait_recv()
        columns = pl.ds(1536 * (1 - part), 768 * (1 + part))
        ograd[:, columns] = (own[xx] + got[0].astype(F32) + got[1].astype(F32)) * 0.125
    def finish(i):
        q = chunk(i)
        arrived_all(rb, 3, q)
        main, last = gather(dmat, rb.at[q])
        picked = jnp.concatenate([main, last], axis=1)
        cols = pl.ds(pl.multiple_of(q * 512, 512), 512)
        otok[:, cols] = (picked[0:128] + picked[128:256] + locb[q]).astype(BF)

    total(0)
    loop(3, finish)
    total(1)
    finish(3)

    def drain(i):
        q = chunk(i)
        sent(sa, 2, q)
        sent(sb, 3, q)
        to_core(s1d, r1d, 0, q).wait_send()
        to_core(s1g, r1g, 1, q).wait_send()

    loop(NQ, drain)
    for part in range(2):
        for k in range(3):
            for hop in hops(part, k):
                hop.wait_send()


def on_device(tokens, routes, gates, keep, cotangent, w_gate, w_up, w_down):
    hbm = pl.BlockSpec(memory_space=pl.ANY)
    vmem = pl.BlockSpec(memory_space=pltpu.VMEM)
    sem = pltpu.SemaphoreType.DMA
    token_grads, expert_grads = pl.pallas_call(
        kernel,
        out_shape=(
            pltpu.VMEM((128, 2048), BF),
            pltpu.VMEM((256, 2304), F32),
        ),
        in_specs=[vmem] * 3 + [hbm] * 5,
        out_specs=(vmem, vmem),
        scratch_shapes=[
            pltpu.VMEM((4, 512, 512), BF),
            pltpu.VMEM((4, 512, 512), BF),
            pltpu.VMEM((4, 128, 512), BF),
            pltpu.VMEM((4, 512, 768), BF),
            pltpu.VMEM((4, 512, 768), BF),
            pltpu.VMEM((4, 768, 512), BF),
            pltpu.VMEM((512, 768), F32),
            pltpu.VMEM((512, 768), F32),
            pltpu.VMEM((512, 768), BF),
            pltpu.VMEM((512, 768), F32),
            pltpu.VMEM((512, 768), BF),
            pltpu.VMEM((512, 768), BF),
            pltpu.VMEM((4, 128, 512), F32),
            pltpu.VMEM((3, 512, 512), BF),
            pltpu.VMEM((4, 256, 512), BF),
            pltpu.VMEM((4, 192, 256), BF),
            pltpu.VMEM((4, 256, 192), BF),
            pltpu.VMEM((4, 512, 384), BF),
            pltpu.VMEM((4, 512, 384), BF),
            pltpu.VMEM((4, 512, 384), BF),
            pltpu.VMEM((4, 512, 384), BF),
            pltpu.VMEM((4, 256, 768), F32),
            pltpu.VMEM((4, 256, 1536), F32),
            pltpu.VMEM((4, 256, 768), BF),
            pltpu.VMEM((4, 256, 1536), BF),
            pltpu.VMEM((4, 256, 768), BF),
            pltpu.VMEM((4, 256, 1536), BF),
            pltpu.VMEM((2, 256, 768), BF),
            pltpu.VMEM((2, 256, 1536), BF),
            pltpu.VMEM((2, 128, 768), BF),
            pltpu.VMEM((2, 128, 1536), BF),
            sem((5, 4)), sem((4, 4)), sem((4, 4, 2)),
            sem((2, 4)), sem((2, 4)), sem((2, 4)), sem((2, 4)),
        ],
        compiler_params=pltpu.CompilerParams(
            collective_id=0, has_side_effects=True, vmem_limit_bytes=60 * 2**20
        ),
    )(routes.T, gates.T, keep.reshape(1, 128), tokens, cotangent, w_gate[0], w_up[0], w_down[0])
    return token_grads, expert_grads[None]


def solution(mesh):
    return jax.shard_map(
        on_device,
        mesh=mesh,
        in_specs=(
            P(("dp", "expert"), None),
            P(("dp", "expert"), None),
            P(("dp", "expert"), None),
            P(("dp", "expert")),
            P(("dp", "expert"), None),
            P("expert", None, None),
            P("expert", None, None),
            P("expert", None, None),
        ),
        out_specs=(P(("dp", "expert"), None), P("expert", "dp", None)),
        check_vma=False,
    )
```

```python
import functools

import jax
import jax.numpy as jnp
from jax import lax
from jax.experimental import pallas as pl
from jax.experimental.pallas import tpu as pltpu
from jax.sharding import PartitionSpec as P

MESH = pl.DeviceIdType.MESH
BF = jnp.bfloat16
F32 = jnp.float32
NQ = 4
ORDER = (1, 7, 3, 5, 2, 6, 4, 0)
SELF = 28


def dot(a, b):
    return jnp.dot(a, b, preferred_element_type=F32)


def dot_nt(a, b):
    return lax.dot_general(a, b, (((1,), (1,)), ((), ())), preferred_element_type=F32)


def dot_tn(a, b):
    return lax.dot_general(a, b, (((0,), (0,)), ((), ())), preferred_element_type=F32)


def onehot(mask):
    return jnp.where(mask, 1.0, 0.0).astype(BF)


def pair(g):
    return pl.ds(256 * g, 256), pl.ds(192 * g, 192)


def iota(shape, axis):
    return lax.broadcasted_iota(jnp.int32, shape, axis)


def loop(n, body):
    def step(i, carry):
        body(i)
        return carry

    lax.fori_loop(0, n, step, 0)


def kernel(
    routes_ref, gates_ref, keep_ref, tok_hbm, cot_hbm, wg_hbm, wu_hbm, wd_hbm,
    otok, ograd,
    xall, call, cot, wg, wu, wd, gacc, uacc, hid, gh, gb, ub, locb,
    lmat, dmat, umat, pmat, sa, ra, sb, rb,
    ownd, owng, s1d, s1g, r1d, r1g, r2d, r2g, hd, hg,
    ld_sem, ssem, rsem, s1s, s1r, s2s, s2r,
):
    me = lax.axis_index("expert")
    dp = lax.axis_index("dp")
    z, y = me // 4, me % 4
    xx, core = dp // 2, dp % 2

    def chunk(i):
        if isinstance(i, int):
            return (xx + (2, 1, 3, 0)[i]) % 4
        return (xx + jnp.where(i == 0, 2, jnp.where(i == 3, 0, 2 * i - 1))) % 4

    def load(part, q):
        cols = pl.ds(pl.multiple_of(q * 512, 512), 512)
        src, dst = (
            (tok_hbm.at[:, cols], xall.at[q, pl.ds(384, 128)]),
            (wg_hbm.at[cols], wg.at[q]),
            (wu_hbm.at[cols], wu.at[q]),
            (wd_hbm.at[:, cols], wd.at[q]),
            (cot_hbm.at[:, cols], cot.at[q]),
        )[part]
        return pltpu.make_async_copy(src, dst, ld_sem.at[part, q])

    for part in range(5):
        for i in range(NQ):
            load(part, chunk(i)).start()

    bar = pltpu.get_barrier_semaphore()
    for i in range(1, 32):
        pl.semaphore_signal(bar, inc=1, device_id={"expert": (me + i) % 32}, device_id_type=MESH)
    for i in range(1, 4):
        pl.semaphore_signal(bar, inc=1, device_id={"dp": ((xx + i) % 4) * 2 + core}, device_id_type=MESH)
    pl.semaphore_signal(bar, inc=1, device_id={"dp": xx * 2 + 1 - core}, device_id_type=MESH)

    lanes = iota((128, 128), 1)
    subs = iota((128, 128), 0)
    eye = lanes == subs

    def column(row):
        return jnp.sum(jnp.where(eye, row, jnp.zeros_like(row)), axis=1, keepdims=True)

    experts = [column(routes_ref[k : k + 1, :].astype(F32)).astype(jnp.int32) for k in range(2)]
    hots = [onehot(lanes == e) for e in experts]
    before = dot(onehot(lanes < subs), hots[0] + hots[1])
    for k in range(2):
        e = experts[k]
        s = jnp.sum(before * hots[k].astype(F32), axis=1, keepdims=True).astype(jnp.int32)
        dz = ((e >> 2) - z) & 7
        dy = ((e & 3) - y) & 3
        turn_of = sum(jnp.where(dz == d, m, 0) for m, d in enumerate(ORDER))
        base = (turn_of * 4 + dy) * 16
        targets = [base + s]
        for j in range(3):
            targets.append(jnp.where((s >> 2) == j, base + 12 + (s & 3), -1))
        rows = []
        for t in range(4):
            dmat[t, pl.ds(128 * k, 128), :] = onehot(iota((128, 512), 1) == targets[t])
            spread = jnp.where(eye, targets[t].astype(F32), 0.0)
            rows.append(jnp.sum(spread, axis=0, keepdims=True).astype(jnp.int32))
        for j in range(3):
            lmat[j, :, pl.ds(256 * k, 128)] = onehot(iota((512, 128), 0) == rows[0])
            lmat[j, :, pl.ds(256 * k + 128, 128)] = onehot(iota((512, 128), 0) == rows[1 + j])

    def exchange(src, dst, a, q, g, sign):
        for p in range(16 * g, 16 * g + 16):
            dz, dy = ORDER[p // 4], p % 4
            block = pl.ds(16 * p, 16)
            if p == SELF:
                pltpu.make_async_copy(src.at[q, block], dst.at[q, block], rsem.at[a, q, g]).start()
            else:
                to = ((z + sign * dz + 8) % 8) * 4 + (y + sign * dy + 4) % 4
                pltpu.make_async_remote_copy(
                    src_ref=src.at[q, block], dst_ref=dst.at[q, block],
                    send_sem=ssem.at[a, q], recv_sem=rsem.at[a, q, g],
                    device_id={"expert": to}, device_id_type=MESH,
                ).start()

    def arrived(dst, a, q, g):
        part = dst.at[q, pair(g)[0]]
        pltpu.make_async_copy(part, part, rsem.at[a, q, g]).wait()

    def arrived_all(dst, a, q):
        arrived(dst, a, q, 0)
        arrived(dst, a, q, 1)

    def sent(src, a, q):
        part = src.at[q, pl.ds(0, 496)]
        pltpu.make_async_copy(part, part, ssem.at[a, q]).wait()

    def scatter(dst, q, first, second):
        for j in range(3):
            part = slice(128 * j, 128 * j + 128)
            stack = jnp.concatenate(
                [first[:, part], first[:, 384:], second[:, part], second[:, 384:]], axis=0
            )
            dst[q, :, part] = dot(lmat[j], stack).astype(BF)

    def gather(mat, src):
        main = dot(mat[0], src[...])
        last = dot(mat[1], src[:, 0:128])
        last += dot(mat[2], src[:, 128:256])
        last += dot(mat[3], src[:, 256:384])
        return main, last

    def unpack(dst, src, q, g):
        packed, plain = pair(g)
        main, last = gather(umat, src.at[q, packed])
        dst[q, plain, 0:384] = main.astype(BF)
        dst[q, plain, 384:512] = last.astype(BF)

    def dispatch(i):
        q = chunk(i)
        load(0, q).wait()
        rows = xall[q, 384:512, :]
        scatter(sa, q, rows, rows)

    loop(NQ, dispatch)
    pl.semaphore_wait(bar, 35)
    for g in range(2):
        loop(NQ, lambda i: exchange(sa, ra, 0, chunk(i), g, 1))

    row = iota((192, 256), 0)
    col = iota((192, 256), 1)
    blk = (row * 43691) >> 19
    s = row - 12 * blk
    umat[0] = onehot(col == 16 * blk + s)
    for j in range(3):
        umat[1 + j] = onehot((col == 16 * blk + 12 + (s & 3)) & ((s >> 2) == j))
    row = iota((256, 192), 0)
    col = iota((256, 192), 1)
    s = row & 15
    pmat[0] = onehot((s < 12) & (col == 12 * (row >> 4) + s))
    for j in range(3):
        pmat[1 + j] = onehot((s >= 12) & (col == 12 * (row >> 4) + 4 * j + s - 12))

    def pack(dst, q, g, rows):
        packed = pair(g)[0]
        for j in range(3):
            part = slice(128 * j, 128 * j + 128)
            dst[q, packed, part] = (dot(pmat[0], rows[:, part]) + dot(pmat[1 + j], rows[:, 384:])).astype(BF)

    gacc[...] = jnp.zeros_like(gacc)
    uacc[...] = jnp.zeros_like(uacc)

    def project(q, rows):
        gacc[rows, :] += dot(xall[q, rows, :], wg[q])
        uacc[rows, :] += dot(xall[q, rows, :], wu[q])

    def activate(r):
        rows = pl.ds(pl.multiple_of(r * 64, 64), 64)
        act = gacc[rows, :]
        hid[rows, :] = (act * jax.nn.sigmoid(act) * uacc[rows, :]).astype(BF)

    def local_in(i):
        q = chunk(i)
        load(1, q).wait()
        load(2, q).wait()
        project(q, pl.ds(384, 128))

    loop(NQ, local_in)
    loop(2, lambda r: activate(r + 6))

    def group(g):
        plain = pair(g)[1]

        def forward_in(i):
            q = chunk(i)
            arrived(ra, 0, q, g)
            unpack(xall, ra, q, g)
            project(q, plain)

        def forward_out(i):
            q = chunk(i)
            if g == 0:
                load(3, q).wait()
            pack(sb, q, g, dot(hid[plain, :], wd[q]).astype(BF))
            exchange(sb, rb, 1, q, g, -1)

        loop(NQ, forward_in)
        loop(3, lambda r: activate(r + 3 * g))
        loop(NQ, forward_out)

    group(0)
    group(1)

    def factors(r):
        rows = pl.ds(pl.multiple_of(r * 64, 64), 64)
        act = gacc[rows, :]
        sigma = jax.nn.sigmoid(act)
        gacc[rows, :] = uacc[rows, :] * (sigma * (1.0 + act * (1.0 - sigma)))
        uacc[rows, :] = act * sigma

    loop(8, factors)

    gates = [column(gates_ref[k : k + 1, :]) for k in range(2)]
    keep = column(keep_ref[...].astype(F32))

    def turn(i):
        q = chunk(i)
        load(4, q).wait()
        local = keep * dot(hid[384:512, :], wd[q])
        sent(sa, 0, q)
        arrived_all(rb, 1, q)
        main, last = gather(dmat, rb.at[q])
        picked = jnp.concatenate([main, last], axis=1)
        mixed = gates[0] * picked[0:128] + gates[1] * picked[128:256]
        difference = mixed - local
        upstream = cot[q].astype(F32) + difference
        scatter(sa, q, (gates[0] * upstream).astype(BF), (gates[1] * upstream).astype(BF))
        exchange(sa, ra, 2, q, 0, 1)
        exchange(sa, ra, 2, q, 1, 1)
        call[q, 384:512, :] = (-(keep * difference)).astype(BF)

    loop(NQ, turn)

    gh[...] = jnp.zeros_like(gh)
    mine = pl.ds(pl.multiple_of(core * 256, 256), 256)
    other = pl.ds(pl.multiple_of((1 - core) * 256, 256), 256)

    def to_core(src, dst, part, q):
        return pltpu.make_async_remote_copy(
            src_ref=src.at[q], dst_ref=dst.at[q], send_sem=s1s.at[part, q], recv_sem=s1r.at[part, q],
            device_id={"dp": xx * 2 + 1 - core}, device_id_type=MESH,
        )

    def to_chip(src, dst, part, n, dx):
        return pltpu.make_async_remote_copy(
            src_ref=src, dst_ref=dst, send_sem=s2s.at[part, n], recv_sem=s2r.at[part, n],
            device_id={"dp": ((xx + dx) % 4) * 2 + core}, device_id_type=MESH,
        )

    low, high = pl.ds(0, 128), pl.ds(128, 128)

    def hops(part, k):
        recv, half, got = ((r1d, hd, r2d), (r1g, hg, r2g))[part]
        block = recv.at[chunk(k)]
        if k == 0:
            return (
                to_chip(block.at[low], half.at[0], part, 0, 1),
                to_chip(block.at[high], half.at[1], part, 1, 3),
            )
        land = got.at[k - 1]
        return tuple(
            to_chip(block.at[rows], land.at[rows], part, 2 * k + n, (1, 3)[k - 1])
            for n, rows in enumerate(((high, low), (low, high))[k - 1])
        )

    def pass_on(part, k):
        own, recv = ((ownd, r1d), (owng, r1g))[part]
        q = chunk(k)
        to_core(recv, recv, part, q).wait_recv()
        if k == 0:
            recv[q] = (own[q] + recv[q].astype(F32)).astype(BF)
            for hop in hops(part, k):
                hop.start()
        else:
            plain, added = ((high, low), (low, high))[k - 1]
            recv[q, plain] = (own[q, plain] + recv[q, plain].astype(F32)).astype(BF)
            hops(part, k)[0].start()
            own[q, added] = own[q, added] + recv[q, added].astype(F32)

    def pass_sum(part, k):
        own, recv, half = ((ownd, r1d, hd), (owng, r1g, hg))[part]
        q = chunk(k)
        added = (low, high)[k - 1]
        hops(part, 0)[k - 1].wait_recv()
        recv[q, added] = (own[q, added] + half[k - 1].astype(F32)).astype(BF)
        hops(part, k)[1].start()

    def down_grads(i):
        q = chunk(i)
        s1d[q] = dot_tn(call[q, :, other], hid[...]).astype(BF)
        to_core(s1d, r1d, 0, q).start()
        ownd[q] = dot_tn(call[q, :, mine], hid[...])

    def hidden_grads(q, rows):
        gh[rows, :] += dot_nt(call[q, rows, :], wd[q])

    def activate_back(r):
        rows = pl.ds(pl.multiple_of(r * 64, 64), 64)
        grad = gh[rows, :]
        gb[rows, :] = (grad * gacc[rows, :]).astype(BF)
        ub[rows, :] = (grad * uacc[rows, :]).astype(BF)

    def backward_in(g, i):
        q = chunk(i)
        arrived(ra, 2, q, g)
        unpack(call, ra, q, g)
        hidden_grads(q, pair(g)[1])

    def backward_out(g, i):
        q = chunk(i)
        plain = pair(g)[1]
        pack(sb, q, g, (dot_nt(gb[plain, :], wg[q]) + dot_nt(ub[plain, :], wu[q])).astype(BF))
        exchange(sb, rb, 3, q, g, -1)

    def weight_grads(i):
        q = chunk(i)
        away = xall[q, :, other]
        s1g[q, :, 0:768] = dot_tn(away, gb[...]).astype(BF)
        s1g[q, :, 768:1536] = dot_tn(away, ub[...]).astype(BF)
        to_core(s1g, r1g, 1, q).start()
        here = xall[q, :, mine]
        owng[q, :, 0:768] = dot_tn(here, gb[...])
        owng[q, :, 768:1536] = dot_tn(here, ub[...])

    loop(NQ, lambda i: hidden_grads(chunk(i), pl.ds(384, 128)))
    loop(2, lambda r: activate_back(r + 6))
    loop(NQ, lambda i: sent(sb, 1, chunk(i)))

    def chunks(i):
        backward_in(0, i)
        backward_in(1, i)
        down_grads(i)
        for k in range(2):
            pl.when(i == k + 1)(functools.partial(pass_on, 0, k))
        pl.when(i == 2)(functools.partial(pass_sum, 0, 1))

    loop(3, chunks)
    pass_on(0, 2)
    pass_sum(0, 2)

    backward_in(0, 3)
    loop(3, activate_back)
    loop(NQ, functools.partial(backward_out, 0))
    backward_in(1, 3)
    loop(3, lambda r: activate_back(r + 3))

    def rest(i):
        weight_grads(i)
        backward_out(1, i)

        @pl.when(i == 0)
        def _():
            down_grads(3)

        for k in range(3):
            pl.when(i == k)(functools.partial(pass_on, 1, k))

    loop(NQ, rest)

    def local_back(i):
        q = chunk(i)
        locb[q] = dot_nt(gb[384:512, :], wg[q]) + dot_nt(ub[384:512, :], wu[q])

    loop(NQ, local_back)
    pass_sum(1, 1)
    pass_sum(1, 2)

    def total(part):
        own, recv, got = ((ownd, r1d, r2d), (owng, r1g, r2g))[part]
        to_core(recv, recv, part, xx).wait_recv()
        own[xx] = own[xx] + recv[xx].astype(F32)
        for hop in hops(part, 1) + hops(part, 2):
            hop.wait_recv()
        columns = pl.ds(1536 * (1 - part), 768 * (1 + part))
        ograd[:, columns] = (own[xx] + got[0].astype(F32) + got[1].astype(F32)) * 0.125
    def finish(i):
        q = chunk(i)
        arrived_all(rb, 3, q)
        main, last = gather(dmat, rb.at[q])
        picked = jnp.concatenate([main, last], axis=1)
        cols = pl.ds(pl.multiple_of(q * 512, 512), 512)
        otok[:, cols] = (picked[0:128] + picked[128:256] + locb[q]).astype(BF)

    total(0)
    loop(3, finish)
    total(1)
    finish(3)

    def drain(i):
        q = chunk(i)
        sent(sa, 2, q)
        sent(sb, 3, q)
        to_core(s1d, r1d, 0, q).wait_send()
        to_core(s1g, r1g, 1, q).wait_send()

    loop(NQ, drain)
    for part in range(2):
        for k in range(3):
            for hop in hops(part, k):
                hop.wait_send()


def on_device(tokens, routes, gates, keep, cotangent, w_gate, w_up, w_down):
    hbm = pl.BlockSpec(memory_space=pl.ANY)
    vmem = pl.BlockSpec(memory_space=pltpu.VMEM)
    sem = pltpu.SemaphoreType.DMA
    token_grads, expert_grads = pl.pallas_call(
        kernel,
        out_shape=(
            pltpu.VMEM((128, 2048), BF),
            pltpu.VMEM((256, 2304), F32),
        ),
        in_specs=[vmem] * 3 + [hbm] * 5,
        out_specs=(vmem, vmem),
        scratch_shapes=[
            pltpu.VMEM((4, 512, 512), BF),
            pltpu.VMEM((4, 512, 512), BF),
            pltpu.VMEM((4, 128, 512), BF),
            pltpu.VMEM((4, 512, 768), BF),
            pltpu.VMEM((4, 512, 768), BF),
            pltpu.VMEM((4, 768, 512), BF),
            pltpu.VMEM((512, 768), F32),
            pltpu.VMEM((512, 768), F32),
            pltpu.VMEM((512, 768), BF),
            pltpu.VMEM((512, 768), F32),
            pltpu.VMEM((512, 768), BF),
            pltpu.VMEM((512, 768), BF),
            pltpu.VMEM((4, 128, 512), F32),
            pltpu.VMEM((3, 512, 512), BF),
            pltpu.VMEM((4, 256, 512), BF),
            pltpu.VMEM((4, 192, 256), BF),
            pltpu.VMEM((4, 256, 192), BF),
            pltpu.VMEM((4, 512, 384), BF),
            pltpu.VMEM((4, 512, 384), BF),
            pltpu.VMEM((4, 512, 384), BF),
            pltpu.VMEM((4, 512, 384), BF),
            pltpu.VMEM((4, 256, 768), F32),
            pltpu.VMEM((4, 256, 1536), F32),
            pltpu.VMEM((4, 256, 768), BF),
            pltpu.VMEM((4, 256, 1536), BF),
            pltpu.VMEM((4, 256, 768), BF),
            pltpu.VMEM((4, 256, 1536), BF),
            pltpu.VMEM((2, 256, 768), BF),
            pltpu.VMEM((2, 256, 1536), BF),
            pltpu.VMEM((2, 128, 768), BF),
            pltpu.VMEM((2, 128, 1536), BF),
            sem((5, 4)), sem((4, 4)), sem((4, 4, 2)),
            sem((2, 4)), sem((2, 4)), sem((2, 6)), sem((2, 6)),
        ],
        compiler_params=pltpu.CompilerParams(
            collective_id=0, has_side_effects=True, vmem_limit_bytes=60 * 2**20
        ),
    )(routes.T, gates.T, keep.reshape(1, 128), tokens, cotangent, w_gate[0], w_up[0], w_down[0])
    return token_grads, expert_grads[None]


def solution(mesh):
    return jax.shard_map(
        on_device,
        mesh=mesh,
        in_specs=(
            P(("dp", "expert"), None),
            P(("dp", "expert"), None),
            P(("dp", "expert"), None),
            P(("dp", "expert")),
            P(("dp", "expert"), None),
            P("expert", None, None),
            P("expert", None, None),
            P("expert", None, None),
        ),
        out_specs=(P(("dp", "expert"), None), P("expert", "dp", None)),
        check_vma=False,
    )
```

```python
import functools

import jax
import jax.numpy as jnp
from jax import lax
from jax.experimental import pallas as pl
from jax.experimental.pallas import tpu as pltpu
from jax.sharding import PartitionSpec as P

MESH = pl.DeviceIdType.MESH
BF = jnp.bfloat16
F32 = jnp.float32
NQ = 4
ORDER = (1, 7, 3, 5, 2, 6, 4, 0)
SELF = 28


def dot(a, b):
    return jnp.dot(a, b, preferred_element_type=F32)


def dot_nt(a, b):
    return lax.dot_general(a, b, (((1,), (1,)), ((), ())), preferred_element_type=F32)


def dot_tn(a, b):
    return lax.dot_general(a, b, (((0,), (0,)), ((), ())), preferred_element_type=F32)


def onehot(mask):
    return jnp.where(mask, 1.0, 0.0).astype(BF)


def pair(g):
    return pl.ds(256 * g, 256), pl.ds(192 * g, 192)


def iota(shape, axis):
    return lax.broadcasted_iota(jnp.int32, shape, axis)


def loop(n, body):
    def step(i, carry):
        body(i)
        return carry

    lax.fori_loop(0, n, step, 0)


def kernel(
    routes_ref, gates_ref, keep_ref, tok_hbm, cot_hbm, wg_hbm, wu_hbm, wd_hbm,
    otok, ograd,
    xall, call, cot, wg, wu, wd, gacc, uacc, hid, gh, gb, ub, locb,
    lmat, dmat, umat, pmat, sa, ra, sb, rb,
    ownd, owng, s1d, s1g, r1d, r1g, r2d, r2g, hd, hg,
    ld_sem, ssem, rsem, s1s, s1r, s2s, s2r,
):
    me = lax.axis_index("expert")
    dp = lax.axis_index("dp")
    z, y = me // 4, me % 4
    xx, core = dp // 2, dp % 2

    def chunk(i):
        if isinstance(i, int):
            return (xx + (2, 1, 3, 0)[i]) % 4
        return (xx + jnp.where(i == 0, 2, jnp.where(i == 3, 0, 2 * i - 1))) % 4

    def load(part, q):
        cols = pl.ds(pl.multiple_of(q * 512, 512), 512)
        src, dst = (
            (tok_hbm.at[:, cols], xall.at[q, pl.ds(384, 128)]),
            (wg_hbm.at[cols], wg.at[q]),
            (wu_hbm.at[cols], wu.at[q]),
            (wd_hbm.at[:, cols], wd.at[q]),
            (cot_hbm.at[:, cols], cot.at[q]),
        )[part]
        return pltpu.make_async_copy(src, dst, ld_sem.at[part, q])

    for part in range(5):
        for i in range(NQ):
            load(part, chunk(i)).start()

    bar = pltpu.get_barrier_semaphore()
    for i in range(1, 32):
        pl.semaphore_signal(bar, inc=1, device_id={"expert": (me + i) % 32}, device_id_type=MESH)
    for i in range(1, 4):
        pl.semaphore_signal(bar, inc=1, device_id={"dp": ((xx + i) % 4) * 2 + core}, device_id_type=MESH)
    pl.semaphore_signal(bar, inc=1, device_id={"dp": xx * 2 + 1 - core}, device_id_type=MESH)

    lanes = iota((128, 128), 1)
    subs = iota((128, 128), 0)
    eye = lanes == subs

    def column(row):
        return jnp.sum(jnp.where(eye, row, jnp.zeros_like(row)), axis=1, keepdims=True)

    experts = [column(routes_ref[k : k + 1, :].astype(F32)).astype(jnp.int32) for k in range(2)]
    hots = [onehot(lanes == e) for e in experts]
    before = dot(onehot(lanes < subs), hots[0] + hots[1])
    for k in range(2):
        e = experts[k]
        s = jnp.sum(before * hots[k].astype(F32), axis=1, keepdims=True).astype(jnp.int32)
        dz = ((e >> 2) - z) & 7
        dy = ((e & 3) - y) & 3
        turn_of = sum(jnp.where(dz == d, m, 0) for m, d in enumerate(ORDER))
        base = (turn_of * 4 + dy) * 16
        targets = [base + s]
        for j in range(3):
            targets.append(jnp.where((s >> 2) == j, base + 12 + (s & 3), -1))
        rows = []
        for t in range(4):
            dmat[t, pl.ds(128 * k, 128), :] = onehot(iota((128, 512), 1) == targets[t])
            spread = jnp.where(eye, targets[t].astype(F32), 0.0)
            rows.append(jnp.sum(spread, axis=0, keepdims=True).astype(jnp.int32))
        for j in range(3):
            lmat[j, :, pl.ds(256 * k, 128)] = onehot(iota((512, 128), 0) == rows[0])
            lmat[j, :, pl.ds(256 * k + 128, 128)] = onehot(iota((512, 128), 0) == rows[1 + j])

    def exchange(src, dst, a, q, g, sign):
        for p in range(16 * g, 16 * g + 16):
            dz, dy = ORDER[p // 4], p % 4
            block = pl.ds(16 * p, 16)
            if p == SELF:
                pltpu.make_async_copy(src.at[q, block], dst.at[q, block], rsem.at[a, q, g]).start()
            else:
                to = ((z + sign * dz + 8) % 8) * 4 + (y + sign * dy + 4) % 4
                pltpu.make_async_remote_copy(
                    src_ref=src.at[q, block], dst_ref=dst.at[q, block],
                    send_sem=ssem.at[a, q], recv_sem=rsem.at[a, q, g],
                    device_id={"expert": to}, device_id_type=MESH,
                ).start()

    def arrived(dst, a, q, g):
        part = dst.at[q, pair(g)[0]]
        pltpu.make_async_copy(part, part, rsem.at[a, q, g]).wait()

    def arrived_all(dst, a, q):
        arrived(dst, a, q, 0)
        arrived(dst, a, q, 1)

    def sent(src, a, q):
        part = src.at[q, pl.ds(0, 496)]
        pltpu.make_async_copy(part, part, ssem.at[a, q]).wait()

    def scatter(dst, q, first, second):
        for j in range(3):
            part = slice(128 * j, 128 * j + 128)
            stack = jnp.concatenate(
                [first[:, part], first[:, 384:], second[:, part], second[:, 384:]], axis=0
            )
            dst[q, :, part] = dot(lmat[j], stack).astype(BF)

    def gather(mat, src):
        main = dot(mat[0], src[...])
        last = dot(mat[1], src[:, 0:128])
        last += dot(mat[2], src[:, 128:256])
        last += dot(mat[3], src[:, 256:384])
        return main, last

    def unpack(dst, src, q, g):
        packed, plain = pair(g)
        main, last = gather(umat, src.at[q, packed])
        dst[q, plain, 0:384] = main.astype(BF)
        dst[q, plain, 384:512] = last.astype(BF)

    def dispatch(i):
        q = chunk(i)
        load(0, q).wait()
        rows = xall[q, 384:512, :]
        scatter(sa, q, rows, rows)

    loop(NQ, dispatch)
    pl.semaphore_wait(bar, 35)
    for g in range(2):
        loop(NQ, lambda i: exchange(sa, ra, 0, chunk(i), g, 1))

    row = iota((192, 256), 0)
    col = iota((192, 256), 1)
    blk = (row * 43691) >> 19
    s = row - 12 * blk
    umat[0] = onehot(col == 16 * blk + s)
    for j in range(3):
        umat[1 + j] = onehot((col == 16 * blk + 12 + (s & 3)) & ((s >> 2) == j))
    row = iota((256, 192), 0)
    col = iota((256, 192), 1)
    s = row & 15
    pmat[0] = onehot((s < 12) & (col == 12 * (row >> 4) + s))
    for j in range(3):
        pmat[1 + j] = onehot((s >= 12) & (col == 12 * (row >> 4) + 4 * j + s - 12))

    def pack(dst, q, g, rows):
        packed = pair(g)[0]
        for j in range(3):
            part = slice(128 * j, 128 * j + 128)
            dst[q, packed, part] = (dot(pmat[0], rows[:, part]) + dot(pmat[1 + j], rows[:, 384:])).astype(BF)

    gacc[...] = jnp.zeros_like(gacc)
    uacc[...] = jnp.zeros_like(uacc)

    def project(q, rows):
        gacc[rows, :] += dot(xall[q, rows, :], wg[q])
        uacc[rows, :] += dot(xall[q, rows, :], wu[q])

    def activate(r):
        rows = pl.ds(pl.multiple_of(r * 64, 64), 64)
        act = gacc[rows, :]
        hid[rows, :] = (act * jax.nn.sigmoid(act) * uacc[rows, :]).astype(BF)

    def local_in(i):
        q = chunk(i)
        load(1, q).wait()
        load(2, q).wait()
        project(q, pl.ds(384, 128))

    loop(NQ, local_in)
    loop(2, lambda r: activate(r + 6))

    def group(g):
        plain = pair(g)[1]

        def forward_in(i):
            q = chunk(i)
            arrived(ra, 0, q, g)
            unpack(xall, ra, q, g)
            project(q, plain)

        def forward_out(i):
            q = chunk(i)
            if g == 0:
                load(3, q).wait()
            pack(sb, q, g, dot(hid[plain, :], wd[q]).astype(BF))
            exchange(sb, rb, 1, q, g, -1)

        loop(NQ, forward_in)
        loop(3, lambda r: activate(r + 3 * g))
        loop(NQ, forward_out)

    group(0)
    group(1)

    def factors(r):
        rows = pl.ds(pl.multiple_of(r * 64, 64), 64)
        act = gacc[rows, :]
        sigma = jax.nn.sigmoid(act)
        gacc[rows, :] = uacc[rows, :] * (sigma * (1.0 + act * (1.0 - sigma)))
        uacc[rows, :] = act * sigma

    loop(8, factors)

    gates = [column(gates_ref[k : k + 1, :]) for k in range(2)]
    keep = column(keep_ref[...].astype(F32))

    def turn(i):
        q = chunk(i)
        load(4, q).wait()
        local = keep * dot(hid[384:512, :], wd[q])
        sent(sa, 0, q)
        arrived_all(rb, 1, q)
        main, last = gather(dmat, rb.at[q])
        picked = jnp.concatenate([main, last], axis=1)
        mixed = gates[0] * picked[0:128] + gates[1] * picked[128:256]
        difference = mixed - local
        upstream = cot[q].astype(F32) + difference
        scatter(sa, q, (gates[0] * upstream).astype(BF), (gates[1] * upstream).astype(BF))
        exchange(sa, ra, 2, q, 0, 1)
        exchange(sa, ra, 2, q, 1, 1)
        call[q, 384:512, :] = (-(keep * difference)).astype(BF)

    loop(NQ, turn)

    gh[...] = jnp.zeros_like(gh)
    mine = pl.ds(pl.multiple_of(core * 256, 256), 256)
    other = pl.ds(pl.multiple_of((1 - core) * 256, 256), 256)

    def to_core(src, dst, part, q):
        return pltpu.make_async_remote_copy(
            src_ref=src.at[q], dst_ref=dst.at[q], send_sem=s1s.at[part, q], recv_sem=s1r.at[part, q],
            device_id={"dp": xx * 2 + 1 - core}, device_id_type=MESH,
        )

    def to_chip(src, dst, part, n, dx):
        return pltpu.make_async_remote_copy(
            src_ref=src, dst_ref=dst, send_sem=s2s.at[part, n], recv_sem=s2r.at[part, n],
            device_id={"dp": ((xx + dx) % 4) * 2 + core}, device_id_type=MESH,
        )

    low, high = pl.ds(0, 128), pl.ds(128, 128)

    def hops(part, k):
        recv, half, got = ((r1d, hd, r2d), (r1g, hg, r2g))[part]
        block = recv.at[chunk(k)]
        if k == 0:
            return (
                to_chip(block.at[low], half.at[0], part, 0, 1),
                to_chip(block.at[high], half.at[1], part, 1, 3),
            )
        land = got.at[k - 1]
        return tuple(
            to_chip(block.at[rows], land.at[rows], part, 2 * k + n, (1, 3)[k - 1])
            for n, rows in enumerate(((high, low), (low, high))[k - 1])
        )

    def pass_on(part, k):
        own, recv = ((ownd, r1d), (owng, r1g))[part]
        q = chunk(k)
        to_core(recv, recv, part, q).wait_recv()
        if k == 0:
            recv[q] = (own[q] + recv[q].astype(F32)).astype(BF)
            for hop in hops(part, k):
                hop.start()
        else:
            plain, added = ((high, low), (low, high))[k - 1]
            recv[q, plain] = (own[q, plain] + recv[q, plain].astype(F32)).astype(BF)
            hops(part, k)[0].start()
            own[q, added] = own[q, added] + recv[q, added].astype(F32)

    def pass_sum(part, k):
        own, recv, half = ((ownd, r1d, hd), (owng, r1g, hg))[part]
        q = chunk(k)
        added = (low, high)[k - 1]
        hops(part, 0)[k - 1].wait_recv()
        recv[q, added] = (own[q, added] + half[k - 1].astype(F32)).astype(BF)
        hops(part, k)[1].start()

    def down_grads(i):
        q = chunk(i)
        s1d[q] = dot_tn(call[q, :, other], hid[...]).astype(BF)
        to_core(s1d, r1d, 0, q).start()
        ownd[q] = dot_tn(call[q, :, mine], hid[...])

    def hidden_grads(q, rows):
        gh[rows, :] += dot_nt(call[q, rows, :], wd[q])

    def activate_back(r):
        rows = pl.ds(pl.multiple_of(r * 64, 64), 64)
        grad = gh[rows, :]
        gb[rows, :] = (grad * gacc[rows, :]).astype(BF)
        ub[rows, :] = (grad * uacc[rows, :]).astype(BF)

    def backward_in(g, i):
        q = chunk(i)
        arrived(ra, 2, q, g)
        unpack(call, ra, q, g)
        hidden_grads(q, pair(g)[1])

    def backward_out(g, i):
        q = chunk(i)
        plain = pair(g)[1]
        pack(sb, q, g, (dot_nt(gb[plain, :], wg[q]) + dot_nt(ub[plain, :], wu[q])).astype(BF))
        exchange(sb, rb, 3, q, g, -1)

    def weight_grads(i):
        q = chunk(i)
        away = xall[q, :, other]
        s1g[q, :, 0:768] = dot_tn(away, gb[...]).astype(BF)
        s1g[q, :, 768:1536] = dot_tn(away, ub[...]).astype(BF)
        to_core(s1g, r1g, 1, q).start()
        here = xall[q, :, mine]
        owng[q, :, 0:768] = dot_tn(here, gb[...])
        owng[q, :, 768:1536] = dot_tn(here, ub[...])

    loop(NQ, lambda i: hidden_grads(chunk(i), pl.ds(384, 128)))
    loop(2, lambda r: activate_back(r + 6))
    loop(NQ, lambda i: sent(sb, 1, chunk(i)))

    def chunks(i):
        backward_in(0, i)
        backward_in(1, i)
        down_grads(i)
        for k in range(2):
            pl.when(i == k + 1)(functools.partial(pass_on, 0, k))
        pl.when(i == 2)(functools.partial(pass_sum, 0, 1))

    loop(3, chunks)
    pass_on(0, 2)
    pass_sum(0, 2)

    backward_in(0, 3)
    loop(3, activate_back)
    loop(2, functools.partial(backward_out, 0))
    backward_in(1, 3)
    loop(3, lambda r: activate_back(r + 3))

    def rest(i):
        weight_grads(i)

        @pl.when(i == 0)
        def _():
            loop(2, lambda n: backward_out(0, n + 2))

        @pl.when(i > 0)
        def _():
            backward_out(1, i)

        for k in range(3):
            pl.when(i == k)(functools.partial(pass_on, 1, k))

        @pl.when(i == 0)
        def _():
            backward_out(1, 0)

    loop(NQ, rest)
    down_grads(3)

    def local_back(i):
        q = chunk(i)
        locb[q] = dot_nt(gb[384:512, :], wg[q]) + dot_nt(ub[384:512, :], wu[q])

    loop(NQ, local_back)
    pass_sum(1, 1)
    pass_sum(1, 2)

    def total(part):
        own, recv, got = ((ownd, r1d, r2d), (owng, r1g, r2g))[part]
        to_core(recv, recv, part, xx).wait_recv()
        own[xx] = own[xx] + recv[xx].astype(F32)
        for hop in hops(part, 1) + hops(part, 2):
            hop.wait_recv()
        columns = pl.ds(1536 * (1 - part), 768 * (1 + part))
        ograd[:, columns] = (own[xx] + got[0].astype(F32) + got[1].astype(F32)) * 0.125
    def finish(i):
        q = chunk(i)
        arrived_all(rb, 3, q)
        main, last = gather(dmat, rb.at[q])
        picked = jnp.concatenate([main, last], axis=1)
        cols = pl.ds(pl.multiple_of(q * 512, 512), 512)
        otok[:, cols] = (picked[0:128] + picked[128:256] + locb[q]).astype(BF)

    total(0)
    loop(NQ, finish)
    total(1)

    def drain(i):
        q = chunk(i)
        sent(sa, 2, q)
        sent(sb, 3, q)
        to_core(s1d, r1d, 0, q).wait_send()
        to_core(s1g, r1g, 1, q).wait_send()

    loop(NQ, drain)
    for part in range(2):
        for k in range(3):
            for hop in hops(part, k):
                hop.wait_send()


def on_device(tokens, routes, gates, keep, cotangent, w_gate, w_up, w_down):
    hbm = pl.BlockSpec(memory_space=pl.ANY)
    vmem = pl.BlockSpec(memory_space=pltpu.VMEM)
    sem = pltpu.SemaphoreType.DMA
    token_grads, expert_grads = pl.pallas_call(
        kernel,
        out_shape=(
            pltpu.VMEM((128, 2048), BF),
            pltpu.VMEM((256, 2304), F32),
        ),
        in_specs=[vmem] * 3 + [hbm] * 5,
        out_specs=(vmem, vmem),
        scratch_shapes=[
            pltpu.VMEM((4, 512, 512), BF),
            pltpu.VMEM((4, 512, 512), BF),
            pltpu.VMEM((4, 128, 512), BF),
            pltpu.VMEM((4, 512, 768), BF),
            pltpu.VMEM((4, 512, 768), BF),
            pltpu.VMEM((4, 768, 512), BF),
            pltpu.VMEM((512, 768), F32),
            pltpu.VMEM((512, 768), F32),
            pltpu.VMEM((512, 768), BF),
            pltpu.VMEM((512, 768), F32),
            pltpu.VMEM((512, 768), BF),
            pltpu.VMEM((512, 768), BF),
            pltpu.VMEM((4, 128, 512), F32),
            pltpu.VMEM((3, 512, 512), BF),
            pltpu.VMEM((4, 256, 512), BF),
            pltpu.VMEM((4, 192, 256), BF),
            pltpu.VMEM((4, 256, 192), BF),
            pltpu.VMEM((4, 512, 384), BF),
            pltpu.VMEM((4, 512, 384), BF),
            pltpu.VMEM((4, 512, 384), BF),
            pltpu.VMEM((4, 512, 384), BF),
            pltpu.VMEM((4, 256, 768), F32),
            pltpu.VMEM((4, 256, 1536), F32),
            pltpu.VMEM((4, 256, 768), BF),
            pltpu.VMEM((4, 256, 1536), BF),
            pltpu.VMEM((4, 256, 768), BF),
            pltpu.VMEM((4, 256, 1536), BF),
            pltpu.VMEM((2, 256, 768), BF),
            pltpu.VMEM((2, 256, 1536), BF),
            pltpu.VMEM((2, 128, 768), BF),
            pltpu.VMEM((2, 128, 1536), BF),
            sem((5, 4)), sem((4, 4)), sem((4, 4, 2)),
            sem((2, 4)), sem((2, 4)), sem((2, 6)), sem((2, 6)),
        ],
        compiler_params=pltpu.CompilerParams(
            collective_id=0, has_side_effects=True, vmem_limit_bytes=60 * 2**20
        ),
    )(routes.T, gates.T, keep.reshape(1, 128), tokens, cotangent, w_gate[0], w_up[0], w_down[0])
    return token_grads, expert_grads[None]


def solution(mesh):
    return jax.shard_map(
        on_device,
        mesh=mesh,
        in_specs=(
            P(("dp", "expert"), None),
            P(("dp", "expert"), None),
            P(("dp", "expert"), None),
            P(("dp", "expert")),
            P(("dp", "expert"), None),
            P("expert", None, None),
            P("expert", None, None),
            P("expert", None, None),
        ),
        out_specs=(P(("dp", "expert"), None), P("expert", "dp", None)),
        check_vma=False,
    )
```
